32 devices in a mesh: side: 4 (over y, x), edge: 8 (over z, core).
Axes of the slice: x: 2, y: 2, z: 4, core: 2. Of those that a mesh axis runs over, the one named last changes fastest.
Arguments:
- parent_blocks: bfloat16 [32, 450, 128], P(('side', 'edge')), may hold values from -6 to 6
- interp_weight: bfloat16 [128, 2, 128, 128], P(('side', 'edge')), may hold values from -0.375 to 0.375
- tile_source: int32 [128, 2], P(('side', 'edge')), may hold values from 0 to 31, as said below
- destination: int32 [16384, 1], P(('side', 'edge')), may hold values from 0 to 7; in each aligned block of 512 rows (0 to 511, 512 to 1023, ...) at most 128 rows name the same one
- remap_matrix: bfloat16 [5, 400, 90], replicated, may hold values from -0.625 to 0.625
Outputs:
- forcing: bfloat16 [5, 400, 32768], P(None, None, ('side', 'edge'))
The draws below stay inside these ranges and needn't reach their ends.
Inputs may be any that keep to these rules, and one draw needn't show every extreme that they name: `tile_source`: the two blocks of a tile are distinct, and each is the tile's own device d or d - 1 or d + 1 modulo 32 along the loop of devices. `destination`: among the rows of one device no owner is named more than 128 times, and in some devices some owner is named exactly 128 times.
All inputs are finite; a program needn't handle non-finite values.
Results may differ from the reference program's by a relative error of at most 0.0049.
Values may be sent and summed in bfloat16 or wider, within the bound.
No kernel may reach another device: no remote copies, remote signals or barrier semaphores. Data moves between devices by JAX's collectives and lax.ppermute only.
A program may use at most 64 MiB of HBM per device.

```python
import math
import jax
import jax.numpy as jnp
import numpy as np
from jax import lax

VARS = 5
LEV_P = 90
LEV_C = 400
PCOL = 128
CROWS = 128
R_DEV = 512
FEAT = 450
TILES = 4
CAP = 128
BLOCKS = 32
SLOTS = 1024
N_SIDE = 4
N_EDGE = 8


def draw_tile_source(key, part):
    total = BLOCKS * TILES
    omitted = jax.random.randint(jax.random.fold_in(key, 11), (total,), 0, 3)
    swapped = jax.random.randint(jax.random.fold_in(key, 12), (total,), 0, 2)
    tile_number = jnp.arange(total, dtype=jnp.int32)
    omitted = jnp.where(tile_number == 0, 2, omitted)
    device = tile_number // TILES
    first = jnp.where(omitted == 0, 0, -1)
    second = jnp.where(omitted == 2, 0, 1)
    lower = (device + first) % BLOCKS
    upper = (device + second) % BLOCKS
    left = jnp.where(swapped == 1, upper, lower)
    right = jnp.where(swapped == 1, lower, upper)
    return jnp.stack([left, right], axis=1).astype(jnp.int32)


def level_of(rng, extent, cuts, least, top_value):
    def one(dim, blocks):
        draws = jax.random.uniform(jax.random.fold_in(jax.random.fold_in(rng, 6), dim), (blocks,), jnp.float32, least / len(cuts), top_value / len(cuts))
        return jnp.repeat(jnp.exp(draws), extent[dim] // blocks).reshape((-1,) + (1,) * (len(extent) - dim - 1))

    factor_of = one(*cuts[0])
    for cut in cuts[1:]:
        factor_of = factor_of * one(*cut)
    return factor_of


def deal_out(key, own, number, rows, count, top, most, skew):
    order = jax.random.permutation(key, count)
    packed, common = portions_of(count, rows * top, most, skew, True), portions_of(count, rows * top, most, skew, False)
    places = jnp.arange(count)

    def named(lengths, offset_by):
        used = int((lengths > 0).sum())
        fixed = max(1, used // 4)
        moved = fixed + (places - fixed + offset_by * (used - fixed)) % max(1, count - fixed)
        return jnp.zeros((count,), jnp.int32).at[order[jnp.where(places < fixed, places, moved)]].set(jnp.asarray(lengths, jnp.int32))

    lengths = jnp.where(number % 4 == 0, named(packed, number // 4), named(common, number - number // 4 - 1))
    mixed = jax.random.permutation(jax.random.fold_in(own, 3), count)
    donor, taker = mixed[0:count // 2 * 2:2], mixed[1:count // 2 * 2:2]
    room = jnp.minimum(lengths[donor] - 1, most - lengths[taker]) // 2
    room = jnp.where((donor == order[0]) | (taker == order[0]) | (lengths[taker] == 0), 0, jnp.maximum(room, 0))
    moved = jax.random.randint(jax.random.fold_in(own, 4), (count // 2,), 0, 1 << 20) % (room + 1)
    lengths = lengths.at[donor].add(-moved).at[taker].add(moved)
    members = jnp.searchsorted(jnp.cumsum(lengths), jnp.arange(rows * top), side="right").astype(jnp.int32)
    grid = members.reshape(top, rows).T
    grid = grid[jax.random.permutation(jax.random.fold_in(own, 1), rows)]
    offset_by = jax.random.randint(jax.random.fold_in(own, 2), (rows, 1), 0, top)
    return jnp.take_along_axis(grid, (jnp.arange(top)[None, :] + offset_by) % top, axis=1)


def portions_of(count, total, bound, lean, full):
    weights = [(1 << 20) // math.isqrt(standing ** lean) + 1 for standing in range(1, count + 1)]
    largest = bound if full else min(bound, max(-(-total // count), total * weights[0] // sum(weights)))
    least = 1 if total - largest >= count - 1 else 0
    counts, rest = [largest] + [least] * (count - 1), total - largest - least * (count - 1)
    while rest > 0:
        movable = [i for i in range(1, count) if counts[i] < largest] or [i for i in range(1, count) if counts[i] < bound]
        whole, budget = sum([weights[i] for i in movable]), rest
        for i in movable:
            addition = min(bound - counts[i], max(1, budget * weights[i] // whole), rest)
            counts[i] = counts[i] + addition
            rest = rest - addition
    return np.array(counts)


def noise(own_key, shape, spread, limit, split=(), held_as=jnp.bfloat16):
    drawn = jax.random.normal(own_key, shape, jnp.float32) * spread
    if len(split) > 0:
        drawn = level_of(own_key, shape, split, -0.22, 0.18) * drawn
    return jnp.clip(drawn, min=-limit, max=limit).astype(held_as)


def setup_inputs(seed: int = 0) -> dict:
    key_list = jax.random.split(jax.random.key(seed), 6)
    parent_blocks = noise(key_list[0], (BLOCKS, FEAT, PCOL), 1.0, 6.0, ((0, 32),))
    interp_weight = noise(key_list[1], (BLOCKS * TILES, 2, PCOL, CROWS), (2 * PCOL) ** -0.5, 0.375, ((0, 32),))
    tile_source = draw_tile_source(jax.random.fold_in(key_list[5], 71), 0)
    destination_keys = jax.random.split(jax.random.fold_in(key_list[3], 1), (BLOCKS * R_DEV) // R_DEV)
    destination_turns = jax.random.permutation(jax.random.fold_in(key_list[3], 3), (BLOCKS * R_DEV) // R_DEV)
    destination = jax.vmap(lambda own, number: deal_out(jax.random.fold_in(key_list[3], 2), own, number, R_DEV, N_EDGE, 1, CAP, 2))(destination_keys, destination_turns).reshape((BLOCKS * R_DEV, 1))
    remap_matrix = noise(key_list[4], (VARS, LEV_C, LEV_P), LEV_P ** -0.5, 0.625)
    return {"parent_blocks": parent_blocks, "interp_weight": interp_weight, "tile_source": tile_source, "destination": destination, "remap_matrix": remap_matrix}


def reference(parent_blocks, interp_weight, tile_source, destination, remap_matrix):
    block_count = N_SIDE * N_EDGE

    def one_tile(inputs):
        sources, weights = inputs
        summed = jnp.dot(parent_blocks[sources[0]], weights[0], preferred_element_type=jnp.float32)
        summed = summed + jnp.dot(parent_blocks[sources[1]], weights[1], preferred_element_type=jnp.float32)
        coarse = lax.optimization_barrier(summed.astype(jnp.bfloat16))
        coarse = coarse.astype(jnp.float32).reshape(VARS, LEV_P, CROWS)
        result = jnp.einsum("vcl,vlr->vcr", remap_matrix.astype(jnp.float32), coarse)
        return result.astype(jnp.bfloat16)

    profiles = lax.map(one_tile, (tile_source, interp_weight))
    profiles = profiles.transpose(1, 2, 0, 3).reshape(VARS, LEV_C, block_count * R_DEV)
    owners = destination[:, 0].reshape(block_count, R_DEV)
    owner_hits = (owners[:, :, None] == jnp.arange(N_EDGE, dtype=jnp.int32)[None, None, :]).astype(jnp.int32)
    places = jnp.sum(jnp.cumsum(owner_hits, axis=1) * owner_hits, axis=2) - 1
    device = jnp.arange(block_count, dtype=jnp.int32)[:, None]
    side_index = device // N_EDGE
    edge_index = device % N_EDGE
    columns = ((side_index * N_EDGE + owners) * SLOTS + edge_index * CAP + places).reshape(-1).astype(jnp.int32)
    forcing = jnp.zeros((VARS, LEV_C, block_count * SLOTS), jnp.bfloat16)
    return forcing.at[:, :, columns].set(profiles)
```

```python
import functools

import jax
import jax.numpy as jnp
from jax import lax
from jax.experimental import pallas as pl
from jax.experimental.pallas import tpu as pltpu
from jax.sharding import PartitionSpec as P

AXES = ("side", "edge")
VMEM = pl.BlockSpec(memory_space=pltpu.VMEM)
SMEM = pl.BlockSpec(memory_space=pltpu.SMEM)


def neighbours(block):
    count = lax.axis_size(AXES)
    up = [(i, (i + 1) % count) for i in range(count)]
    down = [(j, i) for i, j in up]
    return lax.ppermute(block, AXES, up), lax.ppermute(block, AXES, down)


def slot_rows(owner_count, capacity, dest):
    tiles, lanes = dest.shape
    owner = lax.broadcasted_iota(jnp.int32, (owner_count, lanes), 0)
    hits = [(dest[t : t + 1, :] == owner).astype(jnp.float32) for t in range(tiles)]
    earlier = (
        lax.broadcasted_iota(jnp.int32, (lanes, lanes), 0)
        < lax.broadcasted_iota(jnp.int32, (lanes, lanes), 1)
    ).astype(jnp.bfloat16)
    stacked = jnp.concatenate(hits, axis=0).astype(jnp.bfloat16)
    before = jnp.dot(stacked, earlier, preferred_element_type=jnp.float32)
    carry = jnp.zeros((owner_count, 1), jnp.float32)
    slots = []
    for t in range(tiles):
        place = before[t * owner_count : (t + 1) * owner_count, :] + carry
        rank = jnp.sum(hits[t] * place, axis=0, keepdims=True)
        slots.append(dest[t : t + 1, :] * capacity + rank.astype(jnp.int32))
        carry = carry + jnp.sum(hits[t], axis=1, keepdims=True)
    return slots


def select_kernel(sizes, source_ref, dest_ref, weight_ref, out_ref, spread_ref):
    owner_count, capacity, block_count = sizes
    tiles, _, pcol, rows = weight_ref.shape
    position = lax.axis_index("side") * owner_count + lax.axis_index("edge")
    slots = slot_rows(owner_count, capacity, dest_ref[...])
    spread_ref[...] = jnp.zeros_like(spread_ref)
    for t in range(tiles):
        for k in range(2):
            offset = lax.rem(source_ref[k, t] - position + 1 + block_count, block_count)
            place = pl.multiple_of(offset * pcol, pcol)
            spread_ref[pl.ds(place, pcol), t * rows : (t + 1) * rows] = weight_ref[t, k]
    step = 256
    for c in range(owner_count * capacity // step):
        slot = lax.broadcasted_iota(jnp.int32, (step, rows), 0) + c * step
        chosen = jnp.concatenate(
            [(slot == slots[t]).astype(jnp.float32).astype(jnp.bfloat16) for t in range(tiles)],
            axis=1,
        )
        picked = lax.dot_general(
            spread_ref[...], chosen, (((1,), (1,)), ((), ())), preferred_element_type=jnp.float32
        )
        out_ref[:, c * step : (c + 1) * step] = picked.astype(jnp.bfloat16)


def interpolate_kernel(capacity, before_ref, own_ref, after_ref, weight_ref, out_ref):
    parents = jnp.concatenate([before_ref[0], own_ref[0], after_ref[0]], axis=1)
    pair = 2
    for c in range(out_ref.shape[0] // pair):
        width = pair * capacity
        coarse = jnp.dot(
            parents,
            weight_ref[:, c * width : (c + 1) * width],
            preferred_element_type=jnp.float32,
        ).astype(jnp.bfloat16)
        for i in range(pair):
            out_ref[c * pair + i] = coarse[:, i * capacity : (i + 1) * capacity]


def remap_kernel(inbox_ref, remap_ref, out_ref):
    variables, levels, _ = remap_ref.shape
    for v in range(variables):
        rows = jnp.concatenate(
            [inbox_ref[i, v * levels : (v + 1) * levels, :] for i in range(inbox_ref.shape[0])],
            axis=1,
        )
        result = lax.dot_general(
            remap_ref[v], rows, (((0,), (0,)), ((), ())), preferred_element_type=jnp.float32
        )
        out_ref[v] = result.astype(jnp.bfloat16)


def kernel_body(parent_blocks, interp_weight, tile_source, destination, remap_matrix):
    edge_count = lax.axis_size("edge")
    block_count = lax.axis_size(AXES)
    tiles, _, pcol, tile_rows = interp_weight.shape
    features = parent_blocks.shape[1]
    variables, child_levels, levels = remap_matrix.shape
    capacity = 2 * destination.shape[0] // edge_count
    slots = edge_count * capacity

    before, after = neighbours(parent_blocks)
    weights = pl.pallas_call(
        functools.partial(select_kernel, (edge_count, capacity, block_count)),
        out_shape=jax.ShapeDtypeStruct((3 * pcol, slots), jnp.bfloat16),
        in_specs=[SMEM, VMEM, VMEM],
        out_specs=VMEM,
        scratch_shapes=[pltpu.VMEM((3 * pcol, tiles * tile_rows), jnp.bfloat16)],
        cost_estimate=pl.CostEstimate(
            flops=2 * 3 * pcol * tiles * tile_rows * slots,
            bytes_accessed=2 * 3 * pcol * slots,
            transcendentals=0,
        ),
        name="select_weights",
    )(tile_source.T, destination.reshape(tiles, tile_rows), interp_weight)
    outbox = pl.pallas_call(
        functools.partial(interpolate_kernel, capacity),
        out_shape=jax.ShapeDtypeStruct((edge_count, features, capacity), jnp.bfloat16),
        in_specs=[VMEM] * 4,
        out_specs=VMEM,
        cost_estimate=pl.CostEstimate(
            flops=2 * 3 * pcol * features * slots,
            bytes_accessed=2 * features * slots,
            transcendentals=0,
        ),
        name="interpolate",
    )(before, parent_blocks, after, weights)
    inbox = lax.all_to_all(outbox, "edge", split_axis=0, concat_axis=0, tiled=True)
    pair = 2
    return pl.pallas_call(
        remap_kernel,
        grid=(edge_count // pair,),
        out_shape=jax.ShapeDtypeStruct((variables, child_levels, slots), jnp.bfloat16),
        in_specs=[
            pl.BlockSpec((pair, features, capacity), lambda i: (i, 0, 0)),
            pl.BlockSpec((variables, levels, child_levels), lambda i: (0, 0, 0)),
        ],
        out_specs=pl.BlockSpec((variables, child_levels, pair * capacity), lambda i: (0, 0, i)),
        cost_estimate=pl.CostEstimate(
            flops=2 * variables * child_levels * levels * slots,
            bytes_accessed=2 * variables * child_levels * slots,
            transcendentals=0,
        ),
        name="remap",
    )(inbox, jnp.swapaxes(remap_matrix, 1, 2))


def plain_body(parent_blocks, interp_weight, tile_source, destination, remap_matrix):
    edge_count = lax.axis_size("edge")
    block_count = lax.axis_size(AXES)
    position = lax.axis_index(AXES)
    before, after = neighbours(parent_blocks)
    rim_blocks = jnp.concatenate([before, parent_blocks, after], axis=0)
    offset = (tile_source - position + 1 + block_count) % block_count
    chosen = rim_blocks[offset]
    summed = jnp.einsum(
        "tkfp,tkpr->tfr", chosen, interp_weight, preferred_element_type=jnp.float32
    )
    coarse = summed.astype(jnp.bfloat16)
    tile_count, feat_count, tile_rows = coarse.shape
    rows = coarse.transpose(1, 0, 2).reshape(feat_count, tile_count * tile_rows)
    row_count = destination.shape[0]
    capacity = max(2, 2 * row_count // edge_count)
    owners = destination[:, 0]
    owner_hits = (owners[:, None] == jnp.arange(edge_count, dtype=jnp.int32)[None, :]).astype(
        jnp.int32
    )
    places = jnp.sum(jnp.cumsum(owner_hits, axis=0) * owner_hits, axis=1) - 1
    slot_index = owners * capacity + places
    outbox = (
        jnp.zeros((feat_count, edge_count * capacity), jnp.bfloat16).at[:, slot_index].set(rows)
    )
    inbox = lax.all_to_all(outbox, "edge", split_axis=1, concat_axis=1, tiled=True)
    shaped = inbox.reshape(remap_matrix.shape[0], remap_matrix.shape[2], inbox.shape[1])
    result = jnp.einsum("vcl,vln->vcn", remap_matrix, shaped, preferred_element_type=jnp.float32)
    return result.astype(jnp.bfloat16)


def solution(mesh):
    body = kernel_body if mesh.shape["edge"] == 8 else plain_body
    return jax.shard_map(
        body,
        mesh=mesh,
        in_specs=(
            P(AXES, None, None),
            P(AXES, None, None, None),
            P(AXES, None),
            P(AXES, None),
            P(),
        ),
        out_specs=P(None, None, AXES),
        check_vma=False,
    )
```

```python
import functools

import jax
import jax.numpy as jnp
from jax import lax
from jax.experimental import pallas as pl
from jax.experimental.pallas import tpu as pltpu
from jax.sharding import PartitionSpec as P

AXES = ("side", "edge")
VMEM = pl.BlockSpec(memory_space=pltpu.VMEM)
SMEM = pl.BlockSpec(memory_space=pltpu.SMEM)


def neighbours(block):
    count = lax.axis_size(AXES)
    up = [(i, (i + 1) % count) for i in range(count)]
    down = [(j, i) for i, j in up]
    return lax.ppermute(block, AXES, up), lax.ppermute(block, AXES, down)


def slot_rows(owner_count, capacity, dest):
    tiles, lanes = dest.shape
    owner = lax.broadcasted_iota(jnp.int32, (owner_count, lanes), 0)
    hits = [(dest[t : t + 1, :] == owner).astype(jnp.float32) for t in range(tiles)]
    earlier = (
        lax.broadcasted_iota(jnp.int32, (lanes, lanes), 0)
        < lax.broadcasted_iota(jnp.int32, (lanes, lanes), 1)
    ).astype(jnp.bfloat16)
    stacked = jnp.concatenate(hits, axis=0).astype(jnp.bfloat16)
    before = jnp.dot(stacked, earlier, preferred_element_type=jnp.float32)
    carry = jnp.zeros((owner_count, 1), jnp.float32)
    slots = []
    for t in range(tiles):
        place = before[t * owner_count : (t + 1) * owner_count, :] + carry
        rank = jnp.sum(hits[t] * place, axis=0, keepdims=True)
        slots.append(dest[t : t + 1, :] * capacity + rank.astype(jnp.int32))
        carry = carry + jnp.sum(hits[t], axis=1, keepdims=True)
    return slots


def select_kernel(sizes, source_ref, dest_ref, weight_ref, out_ref, spread_ref):
    owner_count, capacity, block_count = sizes
    tiles, _, pcol, rows = weight_ref.shape
    position = lax.axis_index("side") * owner_count + lax.axis_index("edge")
    slots = slot_rows(owner_count, capacity, dest_ref[...])
    spread_ref[...] = jnp.zeros_like(spread_ref)
    for t in range(tiles):
        for k in range(2):
            offset = lax.rem(source_ref[k, t] - position + 1 + block_count, block_count)
            place = pl.multiple_of(offset * pcol, pcol)
            spread_ref[pl.ds(place, pcol), t * rows : (t + 1) * rows] = weight_ref[t, k]
    step = 256
    for c in range(owner_count * capacity // step):
        slot = lax.broadcasted_iota(jnp.int32, (step, rows), 0) + c * step
        chosen = jnp.concatenate(
            [(slot == slots[t]).astype(jnp.float32).astype(jnp.bfloat16) for t in range(tiles)],
            axis=1,
        )
        picked = lax.dot_general(
            spread_ref[...], chosen, (((1,), (1,)), ((), ())), preferred_element_type=jnp.float32
        )
        out_ref[:, c * step : (c + 1) * step] = picked.astype(jnp.bfloat16)


def interpolate_kernel(capacity, before_ref, own_ref, after_ref, weight_ref, out_ref):
    parents = jnp.concatenate([before_ref[0], own_ref[0], after_ref[0]], axis=1)
    pair = 2
    for c in range(out_ref.shape[0] // pair):
        width = pair * capacity
        coarse = jnp.dot(
            parents,
            weight_ref[:, c * width : (c + 1) * width],
            preferred_element_type=jnp.float32,
        ).astype(jnp.bfloat16)
        for i in range(pair):
            out_ref[c * pair + i] = coarse[:, i * capacity : (i + 1) * capacity]


def remap_kernel(inbox_ref, remap_ref, out_ref):
    variables, levels, _ = remap_ref.shape
    for v in range(variables):
        rows = jnp.concatenate(
            [inbox_ref[i, v * levels : (v + 1) * levels, :] for i in range(inbox_ref.shape[0])],
            axis=1,
        )
        result = lax.dot_general(
            remap_ref[v], rows, (((0,), (0,)), ((), ())), preferred_element_type=jnp.float32
        )
        out_ref[v] = result.astype(jnp.bfloat16)


def kernel_body(parent_blocks, interp_weight, tile_source, destination, remap_matrix):
    edge_count = lax.axis_size("edge")
    block_count = lax.axis_size(AXES)
    tiles, _, pcol, tile_rows = interp_weight.shape
    features = parent_blocks.shape[1]
    variables, child_levels, levels = remap_matrix.shape
    capacity = 2 * destination.shape[0] // edge_count
    slots = edge_count * capacity

    before, after = neighbours(parent_blocks)
    weights = pl.pallas_call(
        functools.partial(select_kernel, (edge_count, capacity, block_count)),
        out_shape=jax.ShapeDtypeStruct((3 * pcol, slots), jnp.bfloat16),
        in_specs=[SMEM, VMEM, VMEM],
        out_specs=VMEM,
        scratch_shapes=[pltpu.VMEM((3 * pcol, tiles * tile_rows), jnp.bfloat16)],
        cost_estimate=pl.CostEstimate(
            flops=2 * 3 * pcol * tiles * tile_rows * slots,
            bytes_accessed=2 * 3 * pcol * slots,
            transcendentals=0,
        ),
        name="select_weights", compiler_params=pltpu.CompilerParams(vmem_limit_bytes=16 << 20),
    )(tile_source.T, destination.reshape(tiles, tile_rows), interp_weight)
    outbox = pl.pallas_call(
        functools.partial(interpolate_kernel, capacity),
        out_shape=jax.ShapeDtypeStruct((edge_count, features, capacity), jnp.bfloat16),
        in_specs=[VMEM] * 4,
        out_specs=VMEM,
        cost_estimate=pl.CostEstimate(
            flops=2 * 3 * pcol * features * slots,
            bytes_accessed=2 * features * slots,
            transcendentals=0,
        ),
        name="interpolate", compiler_params=pltpu.CompilerParams(vmem_limit_bytes=16 << 20),
    )(before, parent_blocks, after, weights)
    inbox = lax.all_to_all(outbox, "edge", split_axis=0, concat_axis=0, tiled=True)
    pair = 2
    return pl.pallas_call(
        remap_kernel,
        grid=(edge_count // pair,),
        out_shape=jax.ShapeDtypeStruct((variables, child_levels, slots), jnp.bfloat16),
        in_specs=[
            pl.BlockSpec((pair, features, capacity), lambda i: (i, 0, 0)),
            pl.BlockSpec((variables, levels, child_levels), lambda i: (0, 0, 0)),
        ],
        out_specs=pl.BlockSpec((variables, child_levels, pair * capacity), lambda i: (0, 0, i)),
        cost_estimate=pl.CostEstimate(
            flops=2 * variables * child_levels * levels * slots,
            bytes_accessed=2 * variables * child_levels * slots,
            transcendentals=0,
        ),
        name="remap", compiler_params=pltpu.CompilerParams(vmem_limit_bytes=16 << 20),
    )(inbox, jnp.swapaxes(remap_matrix, 1, 2))


def plain_body(parent_blocks, interp_weight, tile_source, destination, remap_matrix):
    edge_count = lax.axis_size("edge")
    block_count = lax.axis_size(AXES)
    position = lax.axis_index(AXES)
    before, after = neighbours(parent_blocks)
    rim_blocks = jnp.concatenate([before, parent_blocks, after], axis=0)
    offset = (tile_source - position + 1 + block_count) % block_count
    chosen = rim_blocks[offset]
    summed = jnp.einsum(
        "tkfp,tkpr->tfr", chosen, interp_weight, preferred_element_type=jnp.float32
    )
    coarse = summed.astype(jnp.bfloat16)
    tile_count, feat_count, tile_rows = coarse.shape
    rows = coarse.transpose(1, 0, 2).reshape(feat_count, tile_count * tile_rows)
    row_count = destination.shape[0]
    capacity = max(2, 2 * row_count // edge_count)
    owners = destination[:, 0]
    owner_hits = (owners[:, None] == jnp.arange(edge_count, dtype=jnp.int32)[None, :]).astype(
        jnp.int32
    )
    places = jnp.sum(jnp.cumsum(owner_hits, axis=0) * owner_hits, axis=1) - 1
    slot_index = owners * capacity + places
    outbox = (
        jnp.zeros((feat_count, edge_count * capacity), jnp.bfloat16).at[:, slot_index].set(rows)
    )
    inbox = lax.all_to_all(outbox, "edge", split_axis=1, concat_axis=1, tiled=True)
    shaped = inbox.reshape(remap_matrix.shape[0], remap_matrix.shape[2], inbox.shape[1])
    result = jnp.einsum("vcl,vln->vcn", remap_matrix, shaped, preferred_element_type=jnp.float32)
    return result.astype(jnp.bfloat16)


def solution(mesh):
    body = kernel_body if mesh.shape["edge"] == 8 else plain_body
    return jax.shard_map(
        body,
        mesh=mesh,
        in_specs=(
            P(AXES, None, None),
            P(AXES, None, None, None),
            P(AXES, None),
            P(AXES, None),
            P(),
        ),
        out_specs=P(None, None, AXES),
        check_vma=False,
    )
```

```python
import functools

import jax
import jax.numpy as jnp
from jax import lax
from jax.experimental import pallas as pl
from jax.experimental.pallas import tpu as pltpu
from jax.sharding import PartitionSpec as P

AXES = ("side", "edge")
VMEM = pl.BlockSpec(memory_space=pltpu.VMEM)
HBM = pl.BlockSpec(memory_space=pltpu.HBM)
ROOM = pltpu.CompilerParams(vmem_limit_bytes=20 << 20)
WINDOW = 112


def neighbours(block):
    count = lax.axis_size(AXES)
    up = [(i, (i + 1) % count) for i in range(count)]
    down = [(j, i) for i, j in up]
    return lax.ppermute(block, AXES, up), lax.ppermute(block, AXES, down)


def slot_rows(owner_count, capacity, dest):
    tiles, lanes = dest.shape
    owner = lax.broadcasted_iota(jnp.int32, (owner_count, lanes), 0)
    hits = [(dest[t : t + 1, :] == owner).astype(jnp.float32) for t in range(tiles)]
    earlier = (
        lax.broadcasted_iota(jnp.int32, (lanes, lanes), 0)
        < lax.broadcasted_iota(jnp.int32, (lanes, lanes), 1)
    ).astype(jnp.bfloat16)
    stacked = jnp.concatenate(hits, axis=0).astype(jnp.bfloat16)
    before = jnp.dot(stacked, earlier, preferred_element_type=jnp.float32)
    carry = jnp.zeros((owner_count, 1), jnp.float32)
    slots = []
    for t in range(tiles):
        place = before[t * owner_count : (t + 1) * owner_count, :] + carry
        rank = jnp.sum(hits[t] * place, axis=0, keepdims=True)
        slots.append(dest[t : t + 1, :] * capacity + rank.astype(jnp.int32))
        carry = carry + jnp.sum(hits[t], axis=1, keepdims=True)
    return slots


def window_of(v, levels):
    first = v * levels // 16 * 16
    return first, v * levels - first


def select_kernel(sizes, source_hbm, dest_hbm, weight_hbm, out_ref, source, dest, weight, spread, sems):
    owner_count, capacity, block_count = sizes
    tiles, _, pcol, rows = weight.shape
    copies = [
        pltpu.make_async_copy(a, b, sems.at[i])
        for i, (a, b) in enumerate([(dest_hbm, dest), (source_hbm, source), (weight_hbm, weight)])
    ]
    for copy in copies:
        copy.start()
    position = lax.axis_index("side") * owner_count + lax.axis_index("edge")
    copies[0].wait()
    slots = slot_rows(owner_count, capacity, dest[...])
    copies[1].wait()
    copies[2].wait()
    for t in range(tiles):
        first, second = (
            lax.rem(source[k, t] - position + 1 + block_count, block_count) for k in range(2)
        )
        swapped = (first > second).astype(jnp.int32)
        lanes = slice(t * rows, (t + 1) * rows)
        spread[0:pcol, lanes] = weight[t, swapped]
        spread[pcol : 2 * pcol, lanes] = weight[t, 1 - swapped]
        left_out = jnp.full((16, rows), 3 - first - second, jnp.int32)
        spread[2 * pcol : 2 * pcol + 16, lanes] = left_out.astype(jnp.float32).astype(jnp.bfloat16)
    pair = 2
    width = pair * capacity
    height = out_ref.shape[1]
    for c in range(owner_count // pair):
        slot = lax.broadcasted_iota(jnp.int32, (width, rows), 0) + c * width
        chosen = jnp.concatenate(
            [(slot == slots[t]).astype(jnp.float32).astype(jnp.bfloat16) for t in range(tiles)],
            axis=1,
        )
        picked = lax.dot_general(
            spread[...], chosen, (((1,), (1,)), ((), ())), preferred_element_type=jnp.float32
        ).astype(jnp.bfloat16)
        for i in range(pair):
            out_ref[c * pair + i] = picked[:height, i * capacity : (i + 1) * capacity]


def lay_remap_kernel(remap_ref, out_ref):
    variables, levels, child_levels = remap_ref.shape
    for v in range(variables):
        _, place = window_of(v, levels)
        parts = [remap_ref[v].astype(jnp.float32)]
        if place:
            parts.insert(0, jnp.zeros((place, child_levels), jnp.float32))
        parts.append(jnp.zeros((128 - place - levels, child_levels), jnp.float32))
        turned = jnp.concatenate(parts, axis=0).T
        out_ref[v] = turned[:, :WINDOW].astype(jnp.bfloat16)


def join_kernel(own_ref, other_ref, weight_ref, remap_ref, out_ref):
    out_ref[0] = own_ref[0]
    out_ref[1] = other_ref[0]


def collect_kernel(joined_ref, near_ref, held_ref, rim_ref):
    edge = lax.axis_index("edge")
    place, core = edge // 2, lax.rem(edge, 2)
    held_ref[0] = joined_ref[0]
    held_ref[1] = near_ref[0]
    held_ref[2] = joined_ref[1]
    held_ref[3] = near_ref[1]
    rim_ref[0] = held_ref[jnp.bitwise_xor(place, 3 * core)]


def finish_kernel(
    inbox_ref, held_ref, rim_ref, other_ref, other_rim_ref, remap_ref, out_hbm, coarse, result, sems
):
    edge = lax.axis_index("edge")
    place, core = edge // 2, lax.rem(edge, 2)
    variables, child_levels, _ = remap_ref.shape
    features = held_ref.shape[1]
    levels = features // variables
    pcol = held_ref.shape[2]
    capacity = inbox_ref.shape[2]
    chips = inbox_ref.shape[0] // 2

    def block(chip, parity):
        inside = jnp.logical_and(chip >= 0, chip < chips)
        where = jnp.bitwise_and(jnp.bitwise_xor(chip, place), chips - 1)
        mine = jnp.where(inside, held_ref[where], rim_ref[0])
        theirs = jnp.where(inside, other_ref[where], other_rim_ref[0])
        return jnp.where(core == parity, mine, theirs)

    copies = []
    for step in range(chips):
        chip = jnp.bitwise_xor(place, step)
        parents = jnp.concatenate(
            [block(chip - 1, 1), block(chip, 0), block(chip, 1), block(chip + 1, 0)], axis=1
        )
        columns = []
        for parity in range(2):
            sent = inbox_ref.at[2 * chip + parity]
            low, high = sent[0:pcol, :], sent[pcol : 2 * pcol, :]
            left_out = jnp.broadcast_to(sent[2 * pcol : 2 * pcol + 1, :].astype(jnp.float32), (pcol, capacity))
            zero = jnp.zeros_like(low)
            parts = [
                jnp.where(left_out > 0.5, low, zero),
                jnp.where(left_out < 0.5, low, jnp.where(left_out > 1.5, high, zero)),
                jnp.where(left_out < 1.5, high, zero),
            ]
            parts.insert(3 if parity == 0 else 0, zero)
            columns.append(jnp.concatenate(parts, axis=0))
        coarse[step, 0:features, :] = jnp.dot(
            parents, jnp.concatenate(columns, axis=1), preferred_element_type=jnp.float32
        ).astype(jnp.bfloat16)
        rest = coarse.shape[1] - features
        coarse[step, features:, :] = jnp.zeros((rest, 2 * capacity), jnp.bfloat16)
        for v in range(variables):
            first, _ = window_of(v, levels)
            result[step, v] = jnp.dot(
                remap_ref[v],
                coarse[step, first : first + WINDOW, :],
                preferred_element_type=jnp.float32,
            ).astype(jnp.bfloat16)
            slots = pl.ds(pl.multiple_of(chip * 2 * capacity, 2 * capacity), 2 * capacity)
            copy = pltpu.make_async_copy(result.at[step, v], out_hbm.at[v, :, slots], sems.at[step, v])
            copy.start()
            copies.append(copy)
    for copy in copies:
        copy.wait()


def exchange(array, distance):
    count = lax.axis_size("edge")
    return lax.ppermute(array, "edge", [(i, i ^ distance) for i in range(count)])


def across_sides(array):
    sides, count = lax.axis_size("side"), lax.axis_size("edge")
    moves = [
        (s * count + e, (s + (1 if e % 2 else -1)) % sides * count + e)
        for s in range(sides)
        for e in range(count)
    ]
    return lax.ppermute(array, AXES, moves)


def kernel_body(parent_blocks, interp_weight, tile_source, destination, remap_matrix):
    edge_count = lax.axis_size("edge")
    block_count = lax.axis_size(AXES)
    tiles, _, pcol, tile_rows = interp_weight.shape
    features = parent_blocks.shape[1]
    variables, child_levels, levels = remap_matrix.shape
    capacity = 2 * destination.shape[0] // edge_count
    slots = edge_count * capacity
    chips = edge_count // 2
    bf16 = jnp.bfloat16

    def cost(flops, bytes_accessed):
        return pl.CostEstimate(flops=flops, bytes_accessed=bytes_accessed, transcendentals=0)

    far = exchange(parent_blocks, 4)
    height = 2 * pcol + 8
    outbox = pl.pallas_call(
        functools.partial(select_kernel, (edge_count, capacity, block_count)),
        out_shape=jax.ShapeDtypeStruct((edge_count, height, capacity), bf16),
        in_specs=[HBM, HBM, HBM],
        out_specs=VMEM,
        scratch_shapes=[
            pltpu.SMEM((2, tiles), jnp.int32),
            pltpu.VMEM((tiles, tile_rows), jnp.int32),
            pltpu.VMEM(interp_weight.shape, bf16),
            pltpu.VMEM((2 * pcol + 16, tiles * tile_rows), bf16),
            pltpu.SemaphoreType.DMA((3,)),
        ],
        cost_estimate=cost(2 * height * tiles * tile_rows * slots, 2 * height * slots),
        compiler_params=ROOM,
        name="select_weights",
    )(tile_source.T, destination.reshape(tiles, tile_rows), interp_weight)
    inbox = lax.all_to_all(outbox, "edge", split_axis=0, concat_axis=0, tiled=True)
    laid = pl.pallas_call(
        lay_remap_kernel,
        out_shape=jax.ShapeDtypeStruct((variables, child_levels, WINDOW), bf16),
        in_specs=[VMEM],
        out_specs=VMEM,
        compiler_params=ROOM,
        cost_estimate=cost(0, 4 * variables * child_levels * levels),
        name="lay_remap",
    )(jnp.swapaxes(remap_matrix, 1, 2))
    block_bytes = 2 * features * pcol
    joined = pl.pallas_call(
        join_kernel,
        out_shape=jax.ShapeDtypeStruct((2, features, pcol), bf16),
        in_specs=[VMEM, VMEM, pl.BlockSpec(memory_space=pl.ANY), pl.BlockSpec(memory_space=pl.ANY)],
        out_specs=VMEM,
        compiler_params=ROOM,
        cost_estimate=cost(0, 4 * block_bytes),
        name="join",
    )(parent_blocks, far, outbox, laid)
    near = exchange(joined, 2)
    held, rim = pl.pallas_call(
        collect_kernel,
        out_shape=(
            jax.ShapeDtypeStruct((chips, features, pcol), bf16),
            jax.ShapeDtypeStruct((1, features, pcol), bf16),
        ),
        in_specs=[VMEM, VMEM],
        out_specs=(VMEM, VMEM),
        compiler_params=ROOM,
        cost_estimate=cost(0, 9 * block_bytes),
        name="collect",
    )(joined, near)
    rim = across_sides(rim)
    other = exchange(held, 1)
    other_rim = exchange(rim, 1)
    return pl.pallas_call(
        finish_kernel,
        out_shape=jax.ShapeDtypeStruct((variables, child_levels, slots), bf16),
        in_specs=[VMEM] * 6,
        out_specs=HBM,
        scratch_shapes=[
            pltpu.VMEM((chips, 464, 2 * capacity), bf16),
            pltpu.VMEM((chips, variables, child_levels, 2 * capacity), bf16),
            pltpu.SemaphoreType.DMA((chips, variables)),
        ],
        compiler_params=ROOM,
        cost_estimate=cost(
            2 * slots * (4 * pcol * features + variables * child_levels * levels),
            2 * variables * child_levels * slots,
        ),
        name="finish",
    )(inbox, held, rim, other, other_rim, laid)


def plain_body(parent_blocks, interp_weight, tile_source, destination, remap_matrix):
    edge_count = lax.axis_size("edge")
    block_count = lax.axis_size(AXES)
    position = lax.axis_index(AXES)
    before, after = neighbours(parent_blocks)
    rim_blocks = jnp.concatenate([before, parent_blocks, after], axis=0)
    offset = (tile_source - position + 1 + block_count) % block_count
    chosen = rim_blocks[offset]
    summed = jnp.einsum(
        "tkfp,tkpr->tfr", chosen, interp_weight, preferred_element_type=jnp.float32
    )
    coarse = summed.astype(jnp.bfloat16)
    tile_count, feat_count, tile_rows = coarse.shape
    rows = coarse.transpose(1, 0, 2).reshape(feat_count, tile_count * tile_rows)
    row_count = destination.shape[0]
    capacity = max(2, 2 * row_count // edge_count)
    owners = destination[:, 0]
    owner_hits = (owners[:, None] == jnp.arange(edge_count, dtype=jnp.int32)[None, :]).astype(
        jnp.int32
    )
    places = jnp.sum(jnp.cumsum(owner_hits, axis=0) * owner_hits, axis=1) - 1
    slot_index = owners * capacity + places
    outbox = (
        jnp.zeros((feat_count, edge_count * capacity), jnp.bfloat16).at[:, slot_index].set(rows)
    )
    inbox = lax.all_to_all(outbox, "edge", split_axis=1, concat_axis=1, tiled=True)
    shaped = inbox.reshape(remap_matrix.shape[0], remap_matrix.shape[2], inbox.shape[1])
    result = jnp.einsum("vcl,vln->vcn", remap_matrix, shaped, preferred_element_type=jnp.float32)
    return result.astype(jnp.bfloat16)


def solution(mesh):
    body = kernel_body if mesh.shape["edge"] == 8 else plain_body
    return jax.shard_map(
        body,
        mesh=mesh,
        in_specs=(
            P(AXES, None, None),
            P(AXES, None, None, None),
            P(AXES, None),
            P(AXES, None),
            P(),
        ),
        out_specs=P(None, None, AXES),
        check_vma=False,
    )
```

```python
import functools

import jax
import jax.numpy as jnp
from jax import lax
from jax.experimental import pallas as pl
from jax.experimental.pallas import tpu as pltpu
from jax.sharding import PartitionSpec as P

AXES = ("side", "edge")
VMEM = pl.BlockSpec(memory_space=pltpu.VMEM)
HBM = pl.BlockSpec(memory_space=pltpu.HBM)
ANY = pl.BlockSpec(memory_space=pl.ANY)
ROOM = pltpu.CompilerParams(vmem_limit_bytes=20 << 20)
WINDOW = 112


def neighbours(block):
    count = lax.axis_size(AXES)
    up = [(i, (i + 1) % count) for i in range(count)]
    down = [(j, i) for i, j in up]
    return lax.ppermute(block, AXES, up), lax.ppermute(block, AXES, down)


def slot_rows(owner_count, capacity, dest):
    tiles, lanes = dest.shape
    owner = lax.broadcasted_iota(jnp.int32, (owner_count, lanes), 0)
    hits = [(dest[t : t + 1, :] == owner).astype(jnp.float32) for t in range(tiles)]
    earlier = (
        lax.broadcasted_iota(jnp.int32, (lanes, lanes), 0)
        < lax.broadcasted_iota(jnp.int32, (lanes, lanes), 1)
    ).astype(jnp.bfloat16)
    stacked = jnp.concatenate(hits, axis=0).astype(jnp.bfloat16)
    before = jnp.dot(stacked, earlier, preferred_element_type=jnp.float32)
    carry = jnp.zeros((owner_count, 1), jnp.float32)
    slots = []
    for t in range(tiles):
        place = before[t * owner_count : (t + 1) * owner_count, :] + carry
        rank = jnp.sum(hits[t] * place, axis=0, keepdims=True)
        slots.append(dest[t : t + 1, :] * capacity + rank.astype(jnp.int32))
        carry = carry + jnp.sum(hits[t], axis=1, keepdims=True)
    return slots


def window_of(v, levels):
    first = v * levels // 16 * 16
    return first, v * levels - first


def select_kernel(sizes, source_hbm, dest_hbm, weight_hbm, out_ref, source, dest, weight, spread, sems):
    owner_count, capacity, block_count = sizes
    tiles, _, pcol, rows = weight.shape
    copies = [
        pltpu.make_async_copy(a, b, sems.at[i])
        for i, (a, b) in enumerate([(dest_hbm, dest), (source_hbm, source), (weight_hbm, weight)])
    ]
    for copy in copies:
        copy.start()
    position = lax.axis_index("side") * owner_count + lax.axis_index("edge")
    copies[0].wait()
    slots = slot_rows(owner_count, capacity, dest[...])
    copies[1].wait()
    copies[2].wait()
    for t in range(tiles):
        first, second = (
            lax.rem(source[k, t] - position + 1 + block_count, block_count) for k in range(2)
        )
        swapped = (first > second).astype(jnp.int32)
        lanes = slice(t * rows, (t + 1) * rows)
        spread[0:pcol, lanes] = weight[t, swapped]
        spread[pcol : 2 * pcol, lanes] = weight[t, 1 - swapped]
        left_out = jnp.full((16, rows), 3 - first - second, jnp.int32)
        spread[2 * pcol : 2 * pcol + 16, lanes] = left_out.astype(jnp.float32).astype(jnp.bfloat16)
    pair = 2
    width = pair * capacity
    height = out_ref.shape[1]
    for c in range(owner_count // pair):
        slot = lax.broadcasted_iota(jnp.int32, (width, rows), 0) + c * width
        chosen = jnp.concatenate(
            [(slot == slots[t]).astype(jnp.float32).astype(jnp.bfloat16) for t in range(tiles)],
            axis=1,
        )
        picked = lax.dot_general(
            spread[...], chosen, (((1,), (1,)), ((), ())), preferred_element_type=jnp.float32
        ).astype(jnp.bfloat16)
        for i in range(pair):
            out_ref[c * pair + i] = picked[:height, i * capacity : (i + 1) * capacity]


def lay_remap_kernel(remap_ref, out_ref):
    variables, levels, child_levels = remap_ref.shape
    for v in range(variables):
        _, place = window_of(v, levels)
        parts = [remap_ref[v].astype(jnp.float32)]
        if place:
            parts.insert(0, jnp.zeros((place, child_levels), jnp.float32))
        parts.append(jnp.zeros((128 - place - levels, child_levels), jnp.float32))
        turned = jnp.concatenate(parts, axis=0).T
        out_ref[v] = turned[:, :WINDOW].astype(jnp.bfloat16)


def open_join_kernel(own_ref, out_ref):
    out_ref[0] = own_ref[0]


def join_kernel(other_ref, half_ref, out_ref):
    out_ref[0] = half_ref[0]
    out_ref[1] = other_ref[0]


def pass_kernel(laid_ref, joined_ref, out_ref):
    del laid_ref, joined_ref, out_ref


def collect_kernel(joined_ref, near_ref, held_ref, rim_ref):
    edge = lax.axis_index("edge")
    place, core = edge // 2, lax.rem(edge, 2)
    held_ref[0] = joined_ref[0]
    held_ref[1] = near_ref[0]
    held_ref[2] = joined_ref[1]
    held_ref[3] = near_ref[1]
    rim_ref[0] = held_ref[jnp.bitwise_xor(place, 3 * core)]


def finish_kernel(
    inbox_ref, held_ref, rim_ref, other_ref, other_rim_ref, remap_ref, out_hbm, coarse, result, sems
):
    edge = lax.axis_index("edge")
    place, core = edge // 2, lax.rem(edge, 2)
    variables, child_levels, _ = remap_ref.shape
    features = held_ref.shape[1]
    levels = features // variables
    pcol = held_ref.shape[2]
    capacity = inbox_ref.shape[2]
    chips = inbox_ref.shape[0] // 2

    def block(chip, parity):
        inside = jnp.logical_and(chip >= 0, chip < chips)
        where = jnp.bitwise_and(jnp.bitwise_xor(chip, place), chips - 1)
        mine = jnp.where(inside, held_ref[where], rim_ref[0])
        theirs = jnp.where(inside, other_ref[where], other_rim_ref[0])
        return jnp.where(core == parity, mine, theirs)

    copies = []
    for step in range(chips):
        chip = jnp.bitwise_xor(place, step)
        parents = jnp.concatenate(
            [block(chip - 1, 1), block(chip, 0), block(chip, 1), block(chip + 1, 0)], axis=1
        )
        columns = []
        for parity in range(2):
            sent = inbox_ref.at[2 * chip + parity]
            low, high = sent[0:pcol, :], sent[pcol : 2 * pcol, :]
            left_out = jnp.broadcast_to(sent[2 * pcol : 2 * pcol + 1, :].astype(jnp.float32), (pcol, capacity))
            zero = jnp.zeros_like(low)
            parts = [
                jnp.where(left_out > 0.5, low, zero),
                jnp.where(left_out < 0.5, low, jnp.where(left_out > 1.5, high, zero)),
                jnp.where(left_out < 1.5, high, zero),
            ]
            parts.insert(3 if parity == 0 else 0, zero)
            columns.append(jnp.concatenate(parts, axis=0))
        coarse[step, 0:features, :] = jnp.dot(
            parents, jnp.concatenate(columns, axis=1), preferred_element_type=jnp.float32
        ).astype(jnp.bfloat16)
        rest = coarse.shape[1] - features
        coarse[step, features:, :] = jnp.zeros((rest, 2 * capacity), jnp.bfloat16)
        for v in range(variables):
            first, _ = window_of(v, levels)
            result[step, v] = jnp.dot(
                remap_ref[v],
                coarse[step, first : first + WINDOW, :],
                preferred_element_type=jnp.float32,
            ).astype(jnp.bfloat16)
            slots = pl.ds(pl.multiple_of(chip * 2 * capacity, 2 * capacity), 2 * capacity)
            copy = pltpu.make_async_copy(result.at[step, v], out_hbm.at[v, :, slots], sems.at[step, v])
            copy.start()
            copies.append(copy)
    for copy in copies:
        copy.wait()


def exchange(array, distance):
    count = lax.axis_size("edge")
    return lax.ppermute(array, "edge", [(i, i ^ distance) for i in range(count)])


def across_sides(array):
    sides, count = lax.axis_size("side"), lax.axis_size("edge")
    moves = [
        (s * count + e, (s + (1 if e % 2 else -1)) % sides * count + e)
        for s in range(sides)
        for e in range(count)
    ]
    return lax.ppermute(array, AXES, moves)


def kernel_body(parent_blocks, interp_weight, tile_source, destination, remap_matrix):
    edge_count = lax.axis_size("edge")
    block_count = lax.axis_size(AXES)
    tiles, _, pcol, tile_rows = interp_weight.shape
    features = parent_blocks.shape[1]
    variables, child_levels, levels = remap_matrix.shape
    capacity = 2 * destination.shape[0] // edge_count
    slots = edge_count * capacity
    chips = edge_count // 2
    bf16 = jnp.bfloat16

    def cost(flops, bytes_accessed):
        return pl.CostEstimate(flops=flops, bytes_accessed=bytes_accessed, transcendentals=0)

    far = exchange(parent_blocks, 4)
    height = 2 * pcol + 8
    outbox = pl.pallas_call(
        functools.partial(select_kernel, (edge_count, capacity, block_count)),
        out_shape=jax.ShapeDtypeStruct((edge_count, height, capacity), bf16),
        in_specs=[HBM, HBM, HBM],
        out_specs=VMEM,
        scratch_shapes=[
            pltpu.SMEM((2, tiles), jnp.int32),
            pltpu.VMEM((tiles, tile_rows), jnp.int32),
            pltpu.VMEM(interp_weight.shape, bf16),
            pltpu.VMEM((2 * pcol + 16, tiles * tile_rows), bf16),
            pltpu.SemaphoreType.DMA((3,)),
        ],
        cost_estimate=cost(2 * height * tiles * tile_rows * slots, 2 * height * slots),
        name="select_weights",
    )(tile_source.T, destination.reshape(tiles, tile_rows), interp_weight)
    block_bytes = 2 * features * pcol
    laid = pl.pallas_call(
        lay_remap_kernel,
        out_shape=jax.ShapeDtypeStruct((variables, child_levels, WINDOW), bf16),
        in_specs=[VMEM],
        out_specs=VMEM,
        compiler_params=ROOM,
        cost_estimate=cost(0, 4 * variables * child_levels * levels),
        name="lay_remap",
    )(jnp.swapaxes(remap_matrix, 1, 2))
    half = pl.pallas_call(
        open_join_kernel,
        out_shape=jax.ShapeDtypeStruct((2, features, pcol), bf16),
        in_specs=[VMEM],
        out_specs=VMEM,
        compiler_params=ROOM,
        cost_estimate=cost(0, 4 * block_bytes),
        name="open_join",
    )(parent_blocks)
    joined = pl.pallas_call(
        join_kernel,
        out_shape=jax.ShapeDtypeStruct((2, features, pcol), bf16),
        in_specs=[VMEM, VMEM],
        out_specs=VMEM,
        compiler_params=ROOM,
        cost_estimate=cost(0, 2 * block_bytes),
        name="join",
    )(far, half)
    near = exchange(joined, 2)
    laid = pl.pallas_call(
        pass_kernel,
        out_shape=jax.ShapeDtypeStruct(laid.shape, bf16),
        in_specs=[ANY, ANY],
        out_specs=ANY,
        input_output_aliases={0: 0},
        compiler_params=ROOM,
        cost_estimate=cost(10**10, 40000 * variables * child_levels * levels),
        name="behind_join",
    )(laid, joined)
    laid, outbox = lax.optimization_barrier((laid, outbox))
    inbox = lax.all_to_all(outbox, "edge", split_axis=0, concat_axis=0, tiled=True)
    held, rim = pl.pallas_call(
        collect_kernel,
        out_shape=(
            jax.ShapeDtypeStruct((chips, features, pcol), bf16),
            jax.ShapeDtypeStruct((1, features, pcol), bf16),
        ),
        in_specs=[VMEM, VMEM],
        out_specs=(VMEM, VMEM),
        compiler_params=ROOM,
        cost_estimate=cost(10**11, 90000 * block_bytes),
        name="collect",
    )(joined, near)
    rim = across_sides(rim)
    other = exchange(held, 1)
    other_rim = exchange(rim, 1)
    return pl.pallas_call(
        finish_kernel,
        out_shape=jax.ShapeDtypeStruct((variables, child_levels, slots), bf16),
        in_specs=[VMEM] * 6,
        out_specs=HBM,
        scratch_shapes=[
            pltpu.VMEM((chips, 464, 2 * capacity), bf16),
            pltpu.VMEM((chips, variables, child_levels, 2 * capacity), bf16),
            pltpu.SemaphoreType.DMA((chips, variables)),
        ],
        compiler_params=ROOM,
        cost_estimate=cost(
            2 * slots * (4 * pcol * features + variables * child_levels * levels),
            2 * variables * child_levels * slots,
        ),
        name="finish",
    )(inbox, held, rim, other, other_rim, laid)


def plain_body(parent_blocks, interp_weight, tile_source, destination, remap_matrix):
    edge_count = lax.axis_size("edge")
    block_count = lax.axis_size(AXES)
    position = lax.axis_index(AXES)
    before, after = neighbours(parent_blocks)
    rim_blocks = jnp.concatenate([before, parent_blocks, after], axis=0)
    offset = (tile_source - position + 1 + block_count) % block_count
    chosen = rim_blocks[offset]
    summed = jnp.einsum(
        "tkfp,tkpr->tfr", chosen, interp_weight, preferred_element_type=jnp.float32
    )
    coarse = summed.astype(jnp.bfloat16)
    tile_count, feat_count, tile_rows = coarse.shape
    rows = coarse.transpose(1, 0, 2).reshape(feat_count, tile_count * tile_rows)
    row_count = destination.shape[0]
    capacity = max(2, 2 * row_count // edge_count)
    owners = destination[:, 0]
    owner_hits = (owners[:, None] == jnp.arange(edge_count, dtype=jnp.int32)[None, :]).astype(
        jnp.int32
    )
    places = jnp.sum(jnp.cumsum(owner_hits, axis=0) * owner_hits, axis=1) - 1
    slot_index = owners * capacity + places
    outbox = (
        jnp.zeros((feat_count, edge_count * capacity), jnp.bfloat16).at[:, slot_index].set(rows)
    )
    inbox = lax.all_to_all(outbox, "edge", split_axis=1, concat_axis=1, tiled=True)
    shaped = inbox.reshape(remap_matrix.shape[0], remap_matrix.shape[2], inbox.shape[1])
    result = jnp.einsum("vcl,vln->vcn", remap_matrix, shaped, preferred_element_type=jnp.float32)
    return result.astype(jnp.bfloat16)


def solution(mesh):
    body = kernel_body if mesh.shape["edge"] == 8 else plain_body
    return jax.shard_map(
        body,
        mesh=mesh,
        in_specs=(
            P(AXES, None, None),
            P(AXES, None, None, None),
            P(AXES, None),
            P(AXES, None),
            P(),
        ),
        out_specs=P(None, None, AXES),
        check_vma=False,
    )
```

```python
import functools

import jax
import jax.numpy as jnp
from jax import lax
from jax.experimental import pallas as pl
from jax.experimental.pallas import tpu as pltpu
from jax.sharding import PartitionSpec as P

AXES = ("side", "edge")
VMEM = pl.BlockSpec(memory_space=pltpu.VMEM)
HBM = pl.BlockSpec(memory_space=pltpu.HBM)
ANY = pl.BlockSpec(memory_space=pl.ANY)
ROOM = pltpu.CompilerParams(vmem_limit_bytes=20 << 20)
WINDOW = 112


def neighbours(block):
    count = lax.axis_size(AXES)
    up = [(i, (i + 1) % count) for i in range(count)]
    down = [(j, i) for i, j in up]
    return lax.ppermute(block, AXES, up), lax.ppermute(block, AXES, down)


def slot_rows(owner_count, capacity, dest):
    tiles, lanes = dest.shape
    owner = lax.broadcasted_iota(jnp.int32, (owner_count, lanes), 0)
    hits = [(dest[t : t + 1, :] == owner).astype(jnp.float32) for t in range(tiles)]
    earlier = (
        lax.broadcasted_iota(jnp.int32, (lanes, lanes), 0)
        < lax.broadcasted_iota(jnp.int32, (lanes, lanes), 1)
    ).astype(jnp.bfloat16)
    stacked = jnp.concatenate(hits, axis=0).astype(jnp.bfloat16)
    before = jnp.dot(stacked, earlier, preferred_element_type=jnp.float32)
    carry = jnp.zeros((owner_count, 1), jnp.float32)
    slots = []
    for t in range(tiles):
        place = before[t * owner_count : (t + 1) * owner_count, :] + carry
        rank = jnp.sum(hits[t] * place, axis=0, keepdims=True)
        slots.append(dest[t : t + 1, :] * capacity + rank.astype(jnp.int32))
        carry = carry + jnp.sum(hits[t], axis=1, keepdims=True)
    return slots


def window_of(v, levels):
    first = v * levels // 16 * 16
    return first, v * levels - first


def select_kernel(sizes, source_hbm, dest_hbm, weight_hbm, out_ref, source, dest, weight, spread, sems):
    owner_count, capacity, block_count = sizes
    tiles, _, pcol, rows = weight.shape
    copies = [
        pltpu.make_async_copy(a, b, sems.at[i])
        for i, (a, b) in enumerate([(dest_hbm, dest), (source_hbm, source), (weight_hbm, weight)])
    ]
    for copy in copies:
        copy.start()
    position = lax.axis_index("side") * owner_count + lax.axis_index("edge")
    copies[0].wait()
    slots = slot_rows(owner_count, capacity, dest[...])
    copies[1].wait()
    copies[2].wait()
    for t in range(tiles):
        first, second = (
            lax.rem(source[k, t] - position + 1 + block_count, block_count) for k in range(2)
        )
        swapped = (first > second).astype(jnp.int32)
        lanes = slice(t * rows, (t + 1) * rows)
        spread[0:pcol, lanes] = weight[t, swapped]
        spread[pcol : 2 * pcol, lanes] = weight[t, 1 - swapped]
        left_out = jnp.full((16, rows), 3 - first - second, jnp.int32)
        spread[2 * pcol : 2 * pcol + 16, lanes] = left_out.astype(jnp.float32).astype(jnp.bfloat16)
    pair = 2
    width = pair * capacity
    height = out_ref.shape[1]
    for c in range(owner_count // pair):
        slot = lax.broadcasted_iota(jnp.int32, (width, rows), 0) + c * width
        chosen = jnp.concatenate(
            [(slot == slots[t]).astype(jnp.float32).astype(jnp.bfloat16) for t in range(tiles)],
            axis=1,
        )
        picked = lax.dot_general(
            spread[...], chosen, (((1,), (1,)), ((), ())), preferred_element_type=jnp.float32
        ).astype(jnp.bfloat16)
        for i in range(pair):
            out_ref[c * pair + i] = picked[:height, i * capacity : (i + 1) * capacity]


def lay_remap_kernel(remap_ref, out_ref):
    variables, levels, child_levels = remap_ref.shape
    for v in range(variables):
        _, place = window_of(v, levels)
        parts = [remap_ref[v].astype(jnp.float32)]
        if place:
            parts.insert(0, jnp.zeros((place, child_levels), jnp.float32))
        parts.append(jnp.zeros((128 - place - levels, child_levels), jnp.float32))
        turned = jnp.concatenate(parts, axis=0).T
        out_ref[v] = turned[:, :WINDOW].astype(jnp.bfloat16)


def pass_kernel(laid_ref, far_ref, out_ref):
    del laid_ref, far_ref, out_ref


def collect_kernel(own_ref, near_ref, far_ref, last_ref, held_ref, rim_ref):
    edge = lax.axis_index("edge")
    place, core = edge // 2, lax.rem(edge, 2)
    for i, ref in enumerate((own_ref, near_ref, far_ref, last_ref)):
        held_ref[i] = ref[0]
    rim_ref[0] = held_ref[jnp.bitwise_xor(place, 3 * core)]


def finish_kernel(
    inbox_ref, held_ref, rim_ref, other_ref, other_rim_ref, remap_ref, out_hbm, coarse, result, sems
):
    edge = lax.axis_index("edge")
    place, core = edge // 2, lax.rem(edge, 2)
    variables, child_levels, _ = remap_ref.shape
    features = held_ref.shape[1]
    levels = features // variables
    pcol = held_ref.shape[2]
    capacity = inbox_ref.shape[2]
    chips = inbox_ref.shape[0] // 2

    def block(chip, parity):
        inside = jnp.logical_and(chip >= 0, chip < chips)
        where = jnp.bitwise_and(jnp.bitwise_xor(chip, place), chips - 1)
        mine = jnp.where(inside, held_ref[where], rim_ref[0])
        theirs = jnp.where(inside, other_ref[where], other_rim_ref[0])
        return jnp.where(core == parity, mine, theirs)

    copies = []
    for step in range(chips):
        chip = jnp.bitwise_xor(place, step)
        parents = jnp.concatenate(
            [block(chip - 1, 1), block(chip, 0), block(chip, 1), block(chip + 1, 0)], axis=1
        )
        columns = []
        for parity in range(2):
            sent = inbox_ref.at[2 * chip + parity]
            low, high = sent[0:pcol, :], sent[pcol : 2 * pcol, :]
            left_out = jnp.broadcast_to(sent[2 * pcol : 2 * pcol + 1, :].astype(jnp.float32), (pcol, capacity))
            zero = jnp.zeros_like(low)
            parts = [
                jnp.where(left_out > 0.5, low, zero),
                jnp.where(left_out < 0.5, low, jnp.where(left_out > 1.5, high, zero)),
                jnp.where(left_out < 1.5, high, zero),
            ]
            parts.insert(3 if parity == 0 else 0, zero)
            columns.append(jnp.concatenate(parts, axis=0))
        coarse[step, 0:features, :] = jnp.dot(
            parents, jnp.concatenate(columns, axis=1), preferred_element_type=jnp.float32
        ).astype(jnp.bfloat16)
        rest = coarse.shape[1] - features
        coarse[step, features:, :] = jnp.zeros((rest, 2 * capacity), jnp.bfloat16)
        for v in range(variables):
            first, _ = window_of(v, levels)
            result[step, v] = jnp.dot(
                remap_ref[v],
                coarse[step, first : first + WINDOW, :],
                preferred_element_type=jnp.float32,
            ).astype(jnp.bfloat16)
            slots = pl.ds(pl.multiple_of(chip * 2 * capacity, 2 * capacity), 2 * capacity)
            copy = pltpu.make_async_copy(result.at[step, v], out_hbm.at[v, :, slots], sems.at[step, v])
            copy.start()
            copies.append(copy)
    for copy in copies:
        copy.wait()


def exchange(array, distance):
    count = lax.axis_size("edge")
    return lax.ppermute(array, "edge", [(i, i ^ distance) for i in range(count)])


def across_sides(array):
    sides, count = lax.axis_size("side"), lax.axis_size("edge")
    moves = [
        (s * count + e, (s + (1 if e % 2 else -1)) % sides * count + e)
        for s in range(sides)
        for e in range(count)
    ]
    return lax.ppermute(array, AXES, moves)


def kernel_body(parent_blocks, interp_weight, tile_source, destination, remap_matrix):
    edge_count = lax.axis_size("edge")
    block_count = lax.axis_size(AXES)
    tiles, _, pcol, tile_rows = interp_weight.shape
    features = parent_blocks.shape[1]
    variables, child_levels, levels = remap_matrix.shape
    capacity = 2 * destination.shape[0] // edge_count
    slots = edge_count * capacity
    chips = edge_count // 2
    bf16 = jnp.bfloat16

    def cost(flops, bytes_accessed):
        return pl.CostEstimate(flops=flops, bytes_accessed=bytes_accessed, transcendentals=0)

    far = exchange(parent_blocks, 4)
    near = exchange(parent_blocks, 2)
    height = 2 * pcol + 8
    outbox = pl.pallas_call(
        functools.partial(select_kernel, (edge_count, capacity, block_count)),
        out_shape=jax.ShapeDtypeStruct((edge_count, height, capacity), bf16),
        in_specs=[HBM, HBM, HBM],
        out_specs=VMEM,
        scratch_shapes=[
            pltpu.SMEM((2, tiles), jnp.int32),
            pltpu.VMEM((tiles, tile_rows), jnp.int32),
            pltpu.VMEM(interp_weight.shape, bf16),
            pltpu.VMEM((2 * pcol + 16, tiles * tile_rows), bf16),
            pltpu.SemaphoreType.DMA((3,)),
        ],
        cost_estimate=cost(2 * height * tiles * tile_rows * slots, 2 * height * slots),
        name="select_weights",
    )(tile_source.T, destination.reshape(tiles, tile_rows), interp_weight)
    block_bytes = 2 * features * pcol
    laid = pl.pallas_call(
        lay_remap_kernel,
        out_shape=jax.ShapeDtypeStruct((variables, child_levels, WINDOW), bf16),
        in_specs=[VMEM],
        out_specs=VMEM,
        compiler_params=ROOM,
        cost_estimate=cost(0, 4 * variables * child_levels * levels),
        name="lay_remap",
    )(jnp.swapaxes(remap_matrix, 1, 2))
    last = exchange(far, 2)
    laid = pl.pallas_call(
        pass_kernel,
        out_shape=jax.ShapeDtypeStruct(laid.shape, bf16),
        in_specs=[ANY, ANY],
        out_specs=ANY,
        input_output_aliases={0: 0},
        compiler_params=ROOM,
        cost_estimate=cost(10**10, 40000 * variables * child_levels * levels),
        name="behind_last",
    )(laid, far)
    laid, outbox = lax.optimization_barrier((laid, outbox))
    inbox = lax.all_to_all(outbox, "edge", split_axis=0, concat_axis=0, tiled=True)
    held, rim = pl.pallas_call(
        collect_kernel,
        out_shape=(
            jax.ShapeDtypeStruct((chips, features, pcol), bf16),
            jax.ShapeDtypeStruct((1, features, pcol), bf16),
        ),
        in_specs=[VMEM] * 4,
        out_specs=(VMEM, VMEM),
        compiler_params=ROOM,
        cost_estimate=cost(10**11, 90000 * block_bytes),
        name="collect",
    )(parent_blocks, near, far, last)
    rim = across_sides(rim)
    other = exchange(held, 1)
    other_rim = exchange(rim, 1)
    return pl.pallas_call(
        finish_kernel,
        out_shape=jax.ShapeDtypeStruct((variables, child_levels, slots), bf16),
        in_specs=[VMEM] * 6,
        out_specs=HBM,
        scratch_shapes=[
            pltpu.VMEM((chips, 464, 2 * capacity), bf16),
            pltpu.VMEM((chips, variables, child_levels, 2 * capacity), bf16),
            pltpu.SemaphoreType.DMA((chips, variables)),
        ],
        compiler_params=ROOM,
        cost_estimate=cost(
            2 * slots * (4 * pcol * features + variables * child_levels * levels),
            2 * variables * child_levels * slots,
        ),
        name="finish",
    )(inbox, held, rim, other, other_rim, laid)


def plain_body(parent_blocks, interp_weight, tile_source, destination, remap_matrix):
    edge_count = lax.axis_size("edge")
    block_count = lax.axis_size(AXES)
    position = lax.axis_index(AXES)
    before, after = neighbours(parent_blocks)
    rim_blocks = jnp.concatenate([before, parent_blocks, after], axis=0)
    offset = (tile_source - position + 1 + block_count) % block_count
    chosen = rim_blocks[offset]
    summed = jnp.einsum(
        "tkfp,tkpr->tfr", chosen, interp_weight, preferred_element_type=jnp.float32
    )
    coarse = summed.astype(jnp.bfloat16)
    tile_count, feat_count, tile_rows = coarse.shape
    rows = coarse.transpose(1, 0, 2).reshape(feat_count, tile_count * tile_rows)
    row_count = destination.shape[0]
    capacity = max(2, 2 * row_count // edge_count)
    owners = destination[:, 0]
    owner_hits = (owners[:, None] == jnp.arange(edge_count, dtype=jnp.int32)[None, :]).astype(
        jnp.int32
    )
    places = jnp.sum(jnp.cumsum(owner_hits, axis=0) * owner_hits, axis=1) - 1
    slot_index = owners * capacity + places
    outbox = (
        jnp.zeros((feat_count, edge_count * capacity), jnp.bfloat16).at[:, slot_index].set(rows)
    )
    inbox = lax.all_to_all(outbox, "edge", split_axis=1, concat_axis=1, tiled=True)
    shaped = inbox.reshape(remap_matrix.shape[0], remap_matrix.shape[2], inbox.shape[1])
    result = jnp.einsum("vcl,vln->vcn", remap_matrix, shaped, preferred_element_type=jnp.float32)
    return result.astype(jnp.bfloat16)


def solution(mesh):
    body = kernel_body if mesh.shape["edge"] == 8 else plain_body
    return jax.shard_map(
        body,
        mesh=mesh,
        in_specs=(
            P(AXES, None, None),
            P(AXES, None, None, None),
            P(AXES, None),
            P(AXES, None),
            P(),
        ),
        out_specs=P(None, None, AXES),
        check_vma=False,
    )
```

```python
import functools

import jax
import jax.numpy as jnp
from jax import lax
from jax.experimental import pallas as pl
from jax.experimental.pallas import tpu as pltpu
from jax.sharding import PartitionSpec as P

AXES = ("side", "edge")
VMEM = pl.BlockSpec(memory_space=pltpu.VMEM)
HBM = pl.BlockSpec(memory_space=pltpu.HBM)
ANY = pl.BlockSpec(memory_space=pl.ANY)
ROOM = pltpu.CompilerParams(vmem_limit_bytes=20 << 20)
WINDOW = 112


def neighbours(block):
    count = lax.axis_size(AXES)
    up = [(i, (i + 1) % count) for i in range(count)]
    down = [(j, i) for i, j in up]
    return lax.ppermute(block, AXES, up), lax.ppermute(block, AXES, down)


def slot_rows(owner_count, capacity, dest):
    tiles, lanes = dest.shape
    owner = lax.broadcasted_iota(jnp.int32, (owner_count, lanes), 0)
    hits = [(dest[t : t + 1, :] == owner).astype(jnp.float32) for t in range(tiles)]
    earlier = (
        lax.broadcasted_iota(jnp.int32, (lanes, lanes), 0)
        < lax.broadcasted_iota(jnp.int32, (lanes, lanes), 1)
    ).astype(jnp.bfloat16)
    stacked = jnp.concatenate(hits, axis=0).astype(jnp.bfloat16)
    before = jnp.dot(stacked, earlier, preferred_element_type=jnp.float32)
    carry = jnp.zeros((owner_count, 1), jnp.float32)
    slots = []
    for t in range(tiles):
        place = before[t * owner_count : (t + 1) * owner_count, :] + carry
        rank = jnp.sum(hits[t] * place, axis=0, keepdims=True)
        slots.append(dest[t : t + 1, :] * capacity + rank.astype(jnp.int32))
        carry = carry + jnp.sum(hits[t], axis=1, keepdims=True)
    return slots


def window_of(v, levels):
    first = v * levels // 16 * 16
    return first, v * levels - first


def select_kernel(sizes, source_hbm, dest_hbm, weight_hbm, out_ref, source, dest, weight, spread, sems):
    owner_count, capacity, block_count = sizes
    tiles, _, pcol, rows = weight.shape
    copies = [
        pltpu.make_async_copy(a, b, sems.at[i])
        for i, (a, b) in enumerate([(dest_hbm, dest), (source_hbm, source), (weight_hbm, weight)])
    ]
    for copy in copies:
        copy.start()
    position = lax.axis_index("side") * owner_count + lax.axis_index("edge")
    copies[0].wait()
    slots = slot_rows(owner_count, capacity, dest[...])
    copies[1].wait()
    copies[2].wait()
    for t in range(tiles):
        first, second = (
            lax.rem(source[k, t] - position + 1 + block_count, block_count) for k in range(2)
        )
        swapped = (first > second).astype(jnp.int32)
        lanes = slice(t * rows, (t + 1) * rows)
        spread[0:pcol, lanes] = weight[t, swapped]
        spread[pcol : 2 * pcol, lanes] = weight[t, 1 - swapped]
        left_out = jnp.full((16, rows), 3 - first - second, jnp.int32)
        spread[2 * pcol : 2 * pcol + 16, lanes] = left_out.astype(jnp.float32).astype(jnp.bfloat16)
    pair = 2
    width = pair * capacity
    height = out_ref.shape[1]
    for c in range(owner_count // pair):
        slot = lax.broadcasted_iota(jnp.int32, (width, rows), 0) + c * width
        chosen = jnp.concatenate(
            [(slot == slots[t]).astype(jnp.float32).astype(jnp.bfloat16) for t in range(tiles)],
            axis=1,
        )
        picked = lax.dot_general(
            spread[...], chosen, (((1,), (1,)), ((), ())), preferred_element_type=jnp.float32
        ).astype(jnp.bfloat16)
        for i in range(pair):
            out_ref[c * pair + i] = picked[:height, i * capacity : (i + 1) * capacity]


def lay_remap_kernel(remap_ref, out_ref):
    variables, levels, child_levels = remap_ref.shape
    for v in range(variables):
        _, place = window_of(v, levels)
        parts = [remap_ref[v].astype(jnp.float32)]
        if place:
            parts.insert(0, jnp.zeros((place, child_levels), jnp.float32))
        parts.append(jnp.zeros((128 - place - levels, child_levels), jnp.float32))
        turned = jnp.concatenate(parts, axis=0).T
        out_ref[v] = turned[:, :WINDOW].astype(jnp.bfloat16)


def pass_kernel(in_ref, out_ref):
    del in_ref, out_ref


def collect_kernel(own_ref, near_ref, far_ref, last_ref, held_ref, rim_ref):
    edge = lax.axis_index("edge")
    place, core = edge // 2, lax.rem(edge, 2)
    for i, ref in enumerate((own_ref, near_ref, far_ref, last_ref)):
        held_ref[i] = ref[0]
    rim_ref[0] = held_ref[jnp.bitwise_xor(place, 3 * core)]


def finish_kernel(
    inbox_ref, held_ref, rim_ref, other_ref, other_rim_ref, remap_ref, out_hbm, parents, coarse, result, sems
):
    edge = lax.axis_index("edge")
    place, core = edge // 2, lax.rem(edge, 2)
    variables = remap_ref.shape[0]
    features, pcol = held_ref.shape[1:]
    levels = features // variables
    owners, _, capacity = inbox_ref.shape
    chips = owners // 2

    for i in range(owners + 2):
        chip, parity = divmod(i - 1, 2)
        if 0 <= chip < chips:
            where = jnp.bitwise_xor(place, chip)
            mine, theirs = held_ref[where], other_ref[where]
        else:
            mine, theirs = rim_ref[0], other_rim_ref[0]
        parents[0:features, i * pcol : (i + 1) * pcol] = jnp.where(core == parity, mine, theirs)

    def kept(condition):
        return condition.astype(jnp.float32).astype(jnp.bfloat16)

    width = 2 * capacity
    for chip in range(chips):
        columns = []
        for parity in range(2):
            source = 2 * chip + parity
            low, high = inbox_ref[source, 0:pcol, :], inbox_ref[source, pcol : 2 * pcol, :]
            left_out = inbox_ref[source, 2 * pcol : 2 * pcol + 1, :].astype(jnp.float32)
            parts = [
                low * kept(left_out > 0.5),
                low * kept(left_out < 0.5) + high * kept(left_out > 1.5),
                high * kept(left_out < 1.5),
            ]
            parts.insert(3 if parity == 0 else 0, jnp.zeros_like(low))
            columns.append(jnp.concatenate(parts, axis=0))
        coarse[0:features, chip * width : (chip + 1) * width] = jnp.dot(
            parents[0:features, chip * 2 * pcol : (chip * 2 + 4) * pcol],
            jnp.concatenate(columns, axis=1),
            preferred_element_type=jnp.float32,
        ).astype(jnp.bfloat16)
    rest = coarse.shape[0] - features
    coarse[features:, :] = jnp.zeros((rest, owners * capacity), jnp.bfloat16)
    copies = []
    for v in range(variables):
        first, _ = window_of(v, levels)
        for chip in range(chips):
            lanes = slice(chip * width, (chip + 1) * width)
            result[v, :, lanes] = jnp.dot(
                remap_ref[v], coarse[first : first + WINDOW, lanes], preferred_element_type=jnp.float32
            ).astype(jnp.bfloat16)
        copy = pltpu.make_async_copy(result.at[v], out_hbm.at[v], sems.at[v])
        copy.start()
        copies.append(copy)
    for copy in copies:
        copy.wait()


def exchange(array, distance):
    count = lax.axis_size("edge")
    return lax.ppermute(array, "edge", [(i, i ^ distance) for i in range(count)])


def across_sides(array):
    sides, count = lax.axis_size("side"), lax.axis_size("edge")
    moves = [
        (s * count + e, (s + (1 if e % 2 else -1)) % sides * count + e)
        for s in range(sides)
        for e in range(count)
    ]
    return lax.ppermute(array, AXES, moves)


def kernel_body(parent_blocks, interp_weight, tile_source, destination, remap_matrix):
    edge_count = lax.axis_size("edge")
    block_count = lax.axis_size(AXES)
    tiles, _, pcol, tile_rows = interp_weight.shape
    features = parent_blocks.shape[1]
    variables, child_levels, levels = remap_matrix.shape
    capacity = 2 * destination.shape[0] // edge_count
    slots = edge_count * capacity
    chips = edge_count // 2
    bf16 = jnp.bfloat16

    def cost(flops, bytes_accessed):
        return pl.CostEstimate(flops=flops, bytes_accessed=bytes_accessed, transcendentals=0)

    far = exchange(parent_blocks, 4)
    near = exchange(parent_blocks, 2)
    height = 2 * pcol + 8
    outbox = pl.pallas_call(
        functools.partial(select_kernel, (edge_count, capacity, block_count)),
        out_shape=jax.ShapeDtypeStruct((edge_count, height, capacity), bf16),
        in_specs=[HBM, HBM, HBM],
        out_specs=VMEM,
        scratch_shapes=[
            pltpu.SMEM((2, tiles), jnp.int32),
            pltpu.VMEM((tiles, tile_rows), jnp.int32),
            pltpu.VMEM(interp_weight.shape, bf16),
            pltpu.VMEM((2 * pcol + 16, tiles * tile_rows), bf16),
            pltpu.SemaphoreType.DMA((3,)),
        ],
        cost_estimate=cost(2 * height * tiles * tile_rows * slots, 2 * height * slots),
        name="select_weights",
    )(tile_source.T, destination.reshape(tiles, tile_rows), interp_weight)
    block_bytes = 2 * features * pcol
    laid = pl.pallas_call(
        lay_remap_kernel,
        out_shape=jax.ShapeDtypeStruct((variables, child_levels, WINDOW), bf16),
        in_specs=[VMEM],
        out_specs=VMEM,
        compiler_params=ROOM,
        cost_estimate=cost(0, 4 * variables * child_levels * levels),
        name="lay_remap",
    )(jnp.swapaxes(remap_matrix, 1, 2))
    last = exchange(parent_blocks, 6)
    near = pl.pallas_call(
        pass_kernel,
        out_shape=jax.ShapeDtypeStruct(near.shape, bf16),
        in_specs=[ANY],
        out_specs=ANY,
        input_output_aliases={0: 0},
        compiler_params=ROOM,
        cost_estimate=cost(10**10, 10**9),
        name="behind_near",
    )(near)
    near, outbox = lax.optimization_barrier((near, outbox))
    inbox = lax.all_to_all(outbox, "edge", split_axis=0, concat_axis=0, tiled=True)
    held, rim = pl.pallas_call(
        collect_kernel,
        out_shape=(
            jax.ShapeDtypeStruct((chips, features, pcol), bf16),
            jax.ShapeDtypeStruct((1, features, pcol), bf16),
        ),
        in_specs=[VMEM] * 4,
        out_specs=(VMEM, VMEM),
        compiler_params=ROOM,
        cost_estimate=cost(10**11, 90000 * block_bytes),
        name="collect",
    )(parent_blocks, near, far, last)
    rim = across_sides(rim)
    other = exchange(held, 1)
    other_rim = exchange(rim, 1)
    return pl.pallas_call(
        finish_kernel,
        out_shape=jax.ShapeDtypeStruct((variables, child_levels, slots), bf16),
        in_specs=[VMEM] * 6,
        out_specs=HBM,
        scratch_shapes=[
            pltpu.VMEM((464, (edge_count + 2) * pcol), bf16),
            pltpu.VMEM((464, slots), bf16),
            pltpu.VMEM((variables, child_levels, slots), bf16),
            pltpu.SemaphoreType.DMA((variables,)),
        ],
        compiler_params=ROOM,
        cost_estimate=cost(
            2 * slots * (4 * pcol * features + variables * child_levels * levels),
            2 * variables * child_levels * slots,
        ),
        name="finish",
    )(inbox, held, rim, other, other_rim, laid)


def plain_body(parent_blocks, interp_weight, tile_source, destination, remap_matrix):
    edge_count = lax.axis_size("edge")
    block_count = lax.axis_size(AXES)
    position = lax.axis_index(AXES)
    before, after = neighbours(parent_blocks)
    rim_blocks = jnp.concatenate([before, parent_blocks, after], axis=0)
    offset = (tile_source - position + 1 + block_count) % block_count
    chosen = rim_blocks[offset]
    summed = jnp.einsum(
        "tkfp,tkpr->tfr", chosen, interp_weight, preferred_element_type=jnp.float32
    )
    coarse = summed.astype(jnp.bfloat16)
    tile_count, feat_count, tile_rows = coarse.shape
    rows = coarse.transpose(1, 0, 2).reshape(feat_count, tile_count * tile_rows)
    row_count = destination.shape[0]
    capacity = max(2, 2 * row_count // edge_count)
    owners = destination[:, 0]
    owner_hits = (owners[:, None] == jnp.arange(edge_count, dtype=jnp.int32)[None, :]).astype(
        jnp.int32
    )
    places = jnp.sum(jnp.cumsum(owner_hits, axis=0) * owner_hits, axis=1) - 1
    slot_index = owners * capacity + places
    outbox = (
        jnp.zeros((feat_count, edge_count * capacity), jnp.bfloat16).at[:, slot_index].set(rows)
    )
    inbox = lax.all_to_all(outbox, "edge", split_axis=1, concat_axis=1, tiled=True)
    shaped = inbox.reshape(remap_matrix.shape[0], remap_matrix.shape[2], inbox.shape[1])
    result = jnp.einsum("vcl,vln->vcn", remap_matrix, shaped, preferred_element_type=jnp.float32)
    return result.astype(jnp.bfloat16)


def solution(mesh):
    body = kernel_body if mesh.shape["edge"] == 8 else plain_body
    return jax.shard_map(
        body,
        mesh=mesh,
        in_specs=(
            P(AXES, None, None),
            P(AXES, None, None, None),
            P(AXES, None),
            P(AXES, None),
            P(),
        ),
        out_specs=P(None, None, AXES),
        check_vma=False,
    )
```

```python
import functools

import jax
import jax.numpy as jnp
from jax import lax
from jax.experimental import pallas as pl
from jax.experimental.pallas import tpu as pltpu
from jax.sharding import PartitionSpec as P

AXES = ("side", "edge")
VMEM = pl.BlockSpec(memory_space=pltpu.VMEM)
HBM = pl.BlockSpec(memory_space=pltpu.HBM)
ANY = pl.BlockSpec(memory_space=pl.ANY)
ROOM = pltpu.CompilerParams(vmem_limit_bytes=20 << 20)
WINDOW = 112


def neighbours(block):
    count = lax.axis_size(AXES)
    up = [(i, (i + 1) % count) for i in range(count)]
    down = [(j, i) for i, j in up]
    return lax.ppermute(block, AXES, up), lax.ppermute(block, AXES, down)


def slot_rows(owner_count, capacity, dest):
    tiles, lanes = dest.shape
    owner = lax.broadcasted_iota(jnp.int32, (owner_count, lanes), 0)
    hits = [(dest[t : t + 1, :] == owner).astype(jnp.float32) for t in range(tiles)]
    earlier = (
        lax.broadcasted_iota(jnp.int32, (lanes, lanes), 0)
        < lax.broadcasted_iota(jnp.int32, (lanes, lanes), 1)
    ).astype(jnp.bfloat16)
    stacked = jnp.concatenate(hits, axis=0).astype(jnp.bfloat16)
    before = jnp.dot(stacked, earlier, preferred_element_type=jnp.float32)
    carry = jnp.zeros((owner_count, 1), jnp.float32)
    slots = []
    for t in range(tiles):
        place = before[t * owner_count : (t + 1) * owner_count, :] + carry
        rank = jnp.sum(hits[t] * place, axis=0, keepdims=True)
        slots.append(dest[t : t + 1, :] * capacity + rank.astype(jnp.int32))
        carry = carry + jnp.sum(hits[t], axis=1, keepdims=True)
    return slots


def window_of(v, levels):
    first = v * levels // 16 * 16
    return first, v * levels - first


def select_kernel(
    sizes, source_hbm, dest_hbm, weight_hbm, out_ref, kept_ref, given_ref, source, dest, weight, spread, sems
):
    owner_count, capacity, block_count = sizes
    tiles, _, pcol, rows = weight.shape
    copies = [
        pltpu.make_async_copy(a, b, sems.at[i])
        for i, (a, b) in enumerate([(dest_hbm, dest), (source_hbm, source), (weight_hbm, weight)])
    ]
    for copy in copies:
        copy.start()
    position = lax.axis_index("side") * owner_count + lax.axis_index("edge")
    copies[0].wait()
    slots = slot_rows(owner_count, capacity, dest[...])
    copies[1].wait()
    copies[2].wait()
    for t in range(tiles):
        first, second = (
            lax.rem(source[k, t] - position + 1 + block_count, block_count) for k in range(2)
        )
        swapped = (first > second).astype(jnp.int32)
        lanes = slice(t * rows, (t + 1) * rows)
        spread[0:pcol, lanes] = weight[t, swapped]
        spread[pcol : 2 * pcol, lanes] = weight[t, 1 - swapped]
        left_out = jnp.full((16, rows), 3 - first - second, jnp.int32)
        spread[2 * pcol : 2 * pcol + 16, lanes] = left_out.astype(jnp.float32).astype(jnp.bfloat16)
    pair = 2
    width = pair * capacity
    height = out_ref.shape[1]
    for c in range(owner_count // pair):
        slot = lax.broadcasted_iota(jnp.int32, (width, rows), 0) + c * width
        chosen = jnp.concatenate(
            [(slot == slots[t]).astype(jnp.float32).astype(jnp.bfloat16) for t in range(tiles)],
            axis=1,
        )
        picked = lax.dot_general(
            spread[...], chosen, (((1,), (1,)), ((), ())), preferred_element_type=jnp.float32
        ).astype(jnp.bfloat16)
        for i in range(pair):
            out_ref[c * pair + i] = picked[:height, i * capacity : (i + 1) * capacity]
    edge = lax.axis_index("edge")
    kept_ref[...] = out_ref[edge]
    given_ref[...] = out_ref[jnp.bitwise_xor(edge, 1)]


def lay_remap_kernel(remap_ref, out_ref):
    variables, levels, child_levels = remap_ref.shape
    for v in range(variables):
        _, place = window_of(v, levels)
        parts = [remap_ref[v].astype(jnp.float32)]
        if place:
            parts.insert(0, jnp.zeros((place, child_levels), jnp.float32))
        parts.append(jnp.zeros((128 - place - levels, child_levels), jnp.float32))
        turned = jnp.concatenate(parts, axis=0).T
        out_ref[v] = turned[:, :WINDOW].astype(jnp.bfloat16)


def pass_kernel(in_ref, out_ref):
    del in_ref, out_ref


def collect_kernel(own_ref, near_ref, far_ref, last_ref, held_ref, rim_ref):
    edge = lax.axis_index("edge")
    place, core = edge // 2, lax.rem(edge, 2)
    for i, ref in enumerate((own_ref, near_ref, far_ref, last_ref)):
        held_ref[i] = ref[0]
    rim_ref[0] = held_ref[jnp.bitwise_xor(place, 3 * core)]


def spread_weights(rows, parity, pcol):
    def kept(condition):
        return condition.astype(jnp.float32).astype(jnp.bfloat16)

    low, high = rows[0:pcol, :], rows[pcol : 2 * pcol, :]
    left_out = rows[2 * pcol : 2 * pcol + 1, :].astype(jnp.float32)
    parts = [
        low * kept(left_out > 0.5),
        low * kept(left_out < 0.5) + high * kept(left_out > 1.5),
        high * kept(left_out < 1.5),
    ]
    parts.insert(3 if parity == 0 else 0, jnp.zeros_like(low))
    return jnp.concatenate(parts, axis=0)


def begin_kernel(
    own_ref, crossed_ref, held_ref, rim_ref, other_ref, other_rim_ref, remap_ref, parents, begun, coarse
):
    edge = lax.axis_index("edge")
    place, core = edge // 2, lax.rem(edge, 2)
    variables = remap_ref.shape[0]
    chips, features, pcol = held_ref.shape
    levels = features // variables
    owners = 2 * chips

    for i in range(owners + 2):
        chip, parity = divmod(i - 1, 2)
        if 0 <= chip < chips:
            where = jnp.bitwise_xor(place, chip)
            mine, theirs = held_ref[where], other_ref[where]
        else:
            mine, theirs = rim_ref[0], other_rim_ref[0]
        parents[0:features, i * pcol : (i + 1) * pcol] = jnp.where(core == parity, mine, theirs)
    columns = [
        spread_weights(jnp.where(core == parity, own_ref[...], crossed_ref[...]), parity, pcol)
        for parity in range(2)
    ]
    blocks = pl.ds(pl.multiple_of(place * 2 * pcol, 2 * pcol), 4 * pcol)
    coarse[0:features, :] = jnp.dot(
        parents[0:features, blocks],
        jnp.concatenate(columns, axis=1),
        preferred_element_type=jnp.float32,
    ).astype(jnp.bfloat16)
    coarse[features:, :] = jnp.zeros((coarse.shape[0] - features, coarse.shape[1]), jnp.bfloat16)
    for v in range(variables):
        first, _ = window_of(v, levels)
        begun[v] = jnp.dot(
            remap_ref[v], coarse[first : first + WINDOW, :], preferred_element_type=jnp.float32
        ).astype(jnp.bfloat16)


def finish_kernel(levels, inbox_ref, parents_ref, begun_ref, remap_ref, out_hbm, coarse, result, sems):
    place = lax.axis_index("edge") // 2
    variables, child_levels, _ = remap_ref.shape
    owners, _, capacity = inbox_ref.shape
    pcol = parents_ref.shape[1] // (owners + 2)
    features = levels * variables
    width = 2 * capacity
    away = range(1, owners // 2)
    for distance in away:
        chip = jnp.bitwise_xor(place, distance)
        columns = [
            spread_weights(inbox_ref[2 * chip + parity], parity, pcol) for parity in range(2)
        ]
        blocks = pl.ds(pl.multiple_of(chip * 2 * pcol, 2 * pcol), 4 * pcol)
        coarse[0:features, (distance - 1) * width : distance * width] = jnp.dot(
            parents_ref[0:features, blocks],
            jnp.concatenate(columns, axis=1),
            preferred_element_type=jnp.float32,
        ).astype(jnp.bfloat16)
    coarse[features:, :] = jnp.zeros((coarse.shape[0] - features, coarse.shape[1]), jnp.bfloat16)
    copies = []
    for v in range(variables):
        first, _ = window_of(v, levels)
        cuts = [0, child_levels] if v < variables - 1 else [0, child_levels // 32 * 16, child_levels]
        for low, high in zip(cuts[:-1], cuts[1:]):
            for distance in range(owners // 2):
                chip = jnp.bitwise_xor(place, distance)
                lanes = pl.ds(pl.multiple_of(chip * width, width), width)
                if distance == 0:
                    result[v, low:high, lanes] = begun_ref[v, low:high, :]
                else:
                    result[v, low:high, lanes] = jnp.dot(
                        remap_ref[v, low:high, :],
                        coarse[first : first + WINDOW, (distance - 1) * width : distance * width],
                        preferred_element_type=jnp.float32,
                    ).astype(jnp.bfloat16)
            copy = pltpu.make_async_copy(
                result.at[v, low:high], out_hbm.at[v, low:high], sems.at[len(copies)]
            )
            copy.start()
            copies.append(copy)
    for copy in copies:
        copy.wait()


def exchange(array, distance):
    count = lax.axis_size("edge")
    return lax.ppermute(array, "edge", [(i, i ^ distance) for i in range(count)])


def across_sides(array):
    sides, count = lax.axis_size("side"), lax.axis_size("edge")
    moves = [
        (s * count + e, (s + (1 if e % 2 else -1)) % sides * count + e)
        for s in range(sides)
        for e in range(count)
    ]
    return lax.ppermute(array, AXES, moves)


def kernel_body(parent_blocks, interp_weight, tile_source, destination, remap_matrix):
    edge_count = lax.axis_size("edge")
    block_count = lax.axis_size(AXES)
    tiles, _, pcol, tile_rows = interp_weight.shape
    features = parent_blocks.shape[1]
    variables, child_levels, levels = remap_matrix.shape
    capacity = 2 * destination.shape[0] // edge_count
    slots = edge_count * capacity
    chips = edge_count // 2
    bf16 = jnp.bfloat16

    def cost(flops, bytes_accessed):
        return pl.CostEstimate(flops=flops, bytes_accessed=bytes_accessed, transcendentals=0)

    far = exchange(parent_blocks, 4)
    near = exchange(parent_blocks, 2)
    height = 2 * pcol + 8
    outbox, on_chip, given = pl.pallas_call(
        functools.partial(select_kernel, (edge_count, capacity, block_count)),
        out_shape=(
            jax.ShapeDtypeStruct((edge_count, height, capacity), bf16),
            jax.ShapeDtypeStruct((height, capacity), bf16),
            jax.ShapeDtypeStruct((height, capacity), bf16),
        ),
        in_specs=[HBM, HBM, HBM],
        out_specs=(VMEM, VMEM, VMEM),
        scratch_shapes=[
            pltpu.SMEM((2, tiles), jnp.int32),
            pltpu.VMEM((tiles, tile_rows), jnp.int32),
            pltpu.VMEM(interp_weight.shape, bf16),
            pltpu.VMEM((2 * pcol + 16, tiles * tile_rows), bf16),
            pltpu.SemaphoreType.DMA((3,)),
        ],
        cost_estimate=cost(2 * height * tiles * tile_rows * slots, 2 * height * slots),
        name="select_weights",
    )(tile_source.T, destination.reshape(tiles, tile_rows), interp_weight)
    block_bytes = 2 * features * pcol
    laid = pl.pallas_call(
        lay_remap_kernel,
        out_shape=jax.ShapeDtypeStruct((variables, child_levels, WINDOW), bf16),
        in_specs=[VMEM],
        out_specs=VMEM,
        compiler_params=ROOM,
        cost_estimate=cost(0, 4 * variables * child_levels * levels),
        name="lay_remap",
    )(jnp.swapaxes(remap_matrix, 1, 2))
    last = exchange(parent_blocks, 6)
    near = pl.pallas_call(
        pass_kernel,
        out_shape=jax.ShapeDtypeStruct(near.shape, bf16),
        in_specs=[ANY],
        out_specs=ANY,
        input_output_aliases={0: 0},
        compiler_params=ROOM,
        cost_estimate=cost(10**10, 10**9),
        name="behind_near",
    )(near)
    near, outbox = lax.optimization_barrier((near, outbox))
    inbox = lax.all_to_all(outbox, "edge", split_axis=0, concat_axis=0, tiled=True)
    held, rim = pl.pallas_call(
        collect_kernel,
        out_shape=(
            jax.ShapeDtypeStruct((chips, features, pcol), bf16),
            jax.ShapeDtypeStruct((1, features, pcol), bf16),
        ),
        in_specs=[VMEM] * 4,
        out_specs=(VMEM, VMEM),
        compiler_params=ROOM,
        cost_estimate=cost(10**11, 90000 * block_bytes),
        name="collect",
    )(parent_blocks, near, far, last)
    held, given = lax.optimization_barrier((held, given))
    rim = across_sides(rim)
    other = exchange(held, 1)
    other_rim = exchange(rim, 1)
    crossed = exchange(given, 1)
    padded = -(-features // 16) * 16
    parents, begun = pl.pallas_call(
        begin_kernel,
        out_shape=(
            jax.ShapeDtypeStruct((padded, (edge_count + 2) * pcol), bf16),
            jax.ShapeDtypeStruct((variables, child_levels, 2 * capacity), bf16),
        ),
        in_specs=[VMEM] * 7,
        out_specs=(VMEM, VMEM),
        scratch_shapes=[pltpu.VMEM((padded, 2 * capacity), bf16)],
        compiler_params=ROOM,
        cost_estimate=cost(
            4 * capacity * (4 * pcol * features + variables * child_levels * levels),
            2 * variables * child_levels * slots,
        ),
        name="begin",
    )(on_chip, crossed, held, rim, other, other_rim, laid)
    away = slots - 2 * capacity
    return pl.pallas_call(
        functools.partial(finish_kernel, levels),
        out_shape=jax.ShapeDtypeStruct((variables, child_levels, slots), bf16),
        in_specs=[VMEM] * 4,
        out_specs=HBM,
        scratch_shapes=[
            pltpu.VMEM((padded, away), bf16),
            pltpu.VMEM((variables, child_levels, slots), bf16),
            pltpu.SemaphoreType.DMA((variables + 1,)),
        ],
        compiler_params=ROOM,
        cost_estimate=cost(
            2 * away * (4 * pcol * features + variables * child_levels * levels),
            2 * variables * child_levels * slots,
        ),
        name="finish",
    )(inbox, parents, begun, laid)


def plain_body(parent_blocks, interp_weight, tile_source, destination, remap_matrix):
    edge_count = lax.axis_size("edge")
    block_count = lax.axis_size(AXES)
    position = lax.axis_index(AXES)
    before, after = neighbours(parent_blocks)
    rim_blocks = jnp.concatenate([before, parent_blocks, after], axis=0)
    offset = (tile_source - position + 1 + block_count) % block_count
    chosen = rim_blocks[offset]
    summed = jnp.einsum(
        "tkfp,tkpr->tfr", chosen, interp_weight, preferred_element_type=jnp.float32
    )
    coarse = summed.astype(jnp.bfloat16)
    tile_count, feat_count, tile_rows = coarse.shape
    rows = coarse.transpose(1, 0, 2).reshape(feat_count, tile_count * tile_rows)
    row_count = destination.shape[0]
    capacity = max(2, 2 * row_count // edge_count)
    owners = destination[:, 0]
    owner_hits = (owners[:, None] == jnp.arange(edge_count, dtype=jnp.int32)[None, :]).astype(
        jnp.int32
    )
    places = jnp.sum(jnp.cumsum(owner_hits, axis=0) * owner_hits, axis=1) - 1
    slot_index = owners * capacity + places
    outbox = (
        jnp.zeros((feat_count, edge_count * capacity), jnp.bfloat16).at[:, slot_index].set(rows)
    )
    inbox = lax.all_to_all(outbox, "edge", split_axis=1, concat_axis=1, tiled=True)
    shaped = inbox.reshape(remap_matrix.shape[0], remap_matrix.shape[2], inbox.shape[1])
    result = jnp.einsum("vcl,vln->vcn", remap_matrix, shaped, preferred_element_type=jnp.float32)
    return result.astype(jnp.bfloat16)


def solution(mesh):
    body = kernel_body if mesh.shape["edge"] == 8 else plain_body
    return jax.shard_map(
        body,
        mesh=mesh,
        in_specs=(
            P(AXES, None, None),
            P(AXES, None, None, None),
            P(AXES, None),
            P(AXES, None),
            P(),
        ),
        out_specs=P(None, None, AXES),
        check_vma=False,
    )
```

```python
import functools

import jax
import jax.numpy as jnp
from jax import lax
from jax.experimental import pallas as pl
from jax.experimental.pallas import tpu as pltpu
from jax.sharding import PartitionSpec as P

AXES = ("side", "edge")
VMEM = pl.BlockSpec(memory_space=pltpu.VMEM)
HBM = pl.BlockSpec(memory_space=pltpu.HBM)
ANY = pl.BlockSpec(memory_space=pl.ANY)
ROOM = pltpu.CompilerParams(vmem_limit_bytes=20 << 20)
WINDOW = 112


def neighbours(block):
    count = lax.axis_size(AXES)
    up = [(i, (i + 1) % count) for i in range(count)]
    down = [(j, i) for i, j in up]
    return lax.ppermute(block, AXES, up), lax.ppermute(block, AXES, down)


def slot_rows(owner_count, capacity, dest):
    tiles, lanes = dest.shape
    owner = lax.broadcasted_iota(jnp.int32, (owner_count, lanes), 0)
    hits = [(dest[t : t + 1, :] == owner).astype(jnp.float32) for t in range(tiles)]
    earlier = (
        lax.broadcasted_iota(jnp.int32, (lanes, lanes), 0)
        < lax.broadcasted_iota(jnp.int32, (lanes, lanes), 1)
    ).astype(jnp.bfloat16)
    stacked = jnp.concatenate(hits, axis=0).astype(jnp.bfloat16)
    before = jnp.dot(stacked, earlier, preferred_element_type=jnp.float32)
    carry = jnp.zeros((owner_count, 1), jnp.float32)
    slots = []
    for t in range(tiles):
        place = before[t * owner_count : (t + 1) * owner_count, :] + carry
        rank = jnp.sum(hits[t] * place, axis=0, keepdims=True)
        slots.append(dest[t : t + 1, :] * capacity + rank.astype(jnp.int32))
        carry = carry + jnp.sum(hits[t], axis=1, keepdims=True)
    return slots


def window_of(v, levels):
    first = v * levels // 16 * 16
    return first, v * levels - first


def select_kernel(
    sizes, source_hbm, dest_hbm, weight_hbm, out_ref, kept_ref, given_ref, source, dest, weight, spread, sems
):
    owner_count, capacity, block_count = sizes
    tiles, _, pcol, rows = weight.shape
    copies = [
        pltpu.make_async_copy(a, b, sems.at[i])
        for i, (a, b) in enumerate([(dest_hbm, dest), (source_hbm, source), (weight_hbm, weight)])
    ]
    for copy in copies:
        copy.start()
    position = lax.axis_index("side") * owner_count + lax.axis_index("edge")
    copies[0].wait()
    slots = slot_rows(owner_count, capacity, dest[...])
    copies[1].wait()
    copies[2].wait()
    for t in range(tiles):
        first, second = (
            lax.rem(source[k, t] - position + 1 + block_count, block_count) for k in range(2)
        )
        swapped = (first > second).astype(jnp.int32)
        lanes = slice(t * rows, (t + 1) * rows)
        spread[0:pcol, lanes] = weight[t, swapped]
        spread[pcol : 2 * pcol, lanes] = weight[t, 1 - swapped]
        left_out = jnp.full((16, rows), 3 - first - second, jnp.int32)
        spread[2 * pcol : 2 * pcol + 16, lanes] = left_out.astype(jnp.float32).astype(jnp.bfloat16)
    pair = 2
    width = pair * capacity
    height = out_ref.shape[1]
    for c in range(owner_count // pair):
        slot = lax.broadcasted_iota(jnp.int32, (width, rows), 0) + c * width
        chosen = jnp.concatenate(
            [(slot == slots[t]).astype(jnp.float32).astype(jnp.bfloat16) for t in range(tiles)],
            axis=1,
        )
        picked = lax.dot_general(
            spread[...], chosen, (((1,), (1,)), ((), ())), preferred_element_type=jnp.float32
        ).astype(jnp.bfloat16)
        for i in range(pair):
            out_ref[c * pair + i] = picked[:height, i * capacity : (i + 1) * capacity]
    edge = lax.axis_index("edge")
    kept_ref[...] = out_ref[edge]
    given_ref[...] = out_ref[jnp.bitwise_xor(edge, 1)]


def lay_remap_kernel(remap_ref, out_ref):
    variables, levels, child_levels = remap_ref.shape
    for v in range(variables):
        _, place = window_of(v, levels)
        parts = [remap_ref[v].astype(jnp.float32)]
        if place:
            parts.insert(0, jnp.zeros((place, child_levels), jnp.float32))
        parts.append(jnp.zeros((128 - place - levels, child_levels), jnp.float32))
        turned = jnp.concatenate(parts, axis=0).T
        out_ref[v] = turned[:, :WINDOW].astype(jnp.bfloat16)


def pass_kernel(in_ref, out_ref):
    del in_ref, out_ref


def collect_kernel(own_ref, near_ref, far_ref, last_ref, held_ref, rim_ref):
    edge = lax.axis_index("edge")
    place, core = edge // 2, lax.rem(edge, 2)
    for i, ref in enumerate((own_ref, near_ref, far_ref, last_ref)):
        held_ref[i] = ref[0]
    rim_ref[0] = held_ref[jnp.bitwise_xor(place, 3 * core)]


def spread_weights(rows, parity, pcol):
    def kept(condition):
        return condition.astype(jnp.float32).astype(jnp.bfloat16)

    low, high = rows[0:pcol, :], rows[pcol : 2 * pcol, :]
    left_out = rows[2 * pcol : 2 * pcol + 1, :].astype(jnp.float32)
    parts = [
        low * kept(left_out > 0.5),
        low * kept(left_out < 0.5) + high * kept(left_out > 1.5),
        high * kept(left_out < 1.5),
    ]
    parts.insert(3 if parity == 0 else 0, jnp.zeros_like(low))
    return jnp.concatenate(parts, axis=0)


def begin_kernel(
    own_ref,
    crossed_ref,
    held_ref,
    rim_ref,
    other_ref,
    other_rim_ref,
    remap_ref,
    parents,
    out_hbm,
    coarse,
    result,
    sems,
):
    edge = lax.axis_index("edge")
    place, core = edge // 2, lax.rem(edge, 2)
    variables = remap_ref.shape[0]
    chips, features, pcol = held_ref.shape
    levels = features // variables
    owners = 2 * chips

    for i in range(owners + 2):
        chip, parity = divmod(i - 1, 2)
        if 0 <= chip < chips:
            where = jnp.bitwise_xor(place, chip)
            mine, theirs = held_ref[where], other_ref[where]
        else:
            mine, theirs = rim_ref[0], other_rim_ref[0]
        parents[0:features, i * pcol : (i + 1) * pcol] = jnp.where(core == parity, mine, theirs)
    columns = [
        spread_weights(jnp.where(core == parity, own_ref[...], crossed_ref[...]), parity, pcol)
        for parity in range(2)
    ]
    blocks = pl.ds(pl.multiple_of(place * 2 * pcol, 2 * pcol), 4 * pcol)
    coarse[0:features, :] = jnp.dot(
        parents[0:features, blocks],
        jnp.concatenate(columns, axis=1),
        preferred_element_type=jnp.float32,
    ).astype(jnp.bfloat16)
    coarse[features:, :] = jnp.zeros((coarse.shape[0] - features, coarse.shape[1]), jnp.bfloat16)
    slots = pl.ds(pl.multiple_of(place * coarse.shape[1], coarse.shape[1]), coarse.shape[1])
    copies = []
    for v in range(variables):
        first, _ = window_of(v, levels)
        result[v] = jnp.dot(
            remap_ref[v], coarse[first : first + WINDOW, :], preferred_element_type=jnp.float32
        ).astype(jnp.bfloat16)
        copy = pltpu.make_async_copy(result.at[v], out_hbm.at[v, :, slots], sems.at[v])
        copy.start()
        copies.append(copy)
    for copy in copies:
        copy.wait()


def finish_kernel(levels, inbox_ref, parents_ref, remap_ref, begun_hbm, out_hbm, coarse, result, sems):
    del begun_hbm
    place = lax.axis_index("edge") // 2
    variables = remap_ref.shape[0]
    owners, _, capacity = inbox_ref.shape
    pcol = parents_ref.shape[1] // (owners + 2)
    features = levels * variables
    width = 2 * capacity
    away = range(1, owners // 2)
    for distance in away:
        chip = jnp.bitwise_xor(place, distance)
        columns = [
            spread_weights(inbox_ref[2 * chip + parity], parity, pcol) for parity in range(2)
        ]
        blocks = pl.ds(pl.multiple_of(chip * 2 * pcol, 2 * pcol), 4 * pcol)
        coarse[0:features, (distance - 1) * width : distance * width] = jnp.dot(
            parents_ref[0:features, blocks],
            jnp.concatenate(columns, axis=1),
            preferred_element_type=jnp.float32,
        ).astype(jnp.bfloat16)
    coarse[features:, :] = jnp.zeros((coarse.shape[0] - features, coarse.shape[1]), jnp.bfloat16)
    copies = []
    for v in range(variables):
        first, _ = window_of(v, levels)
        for distance in away:
            result[distance - 1, v] = jnp.dot(
                remap_ref[v],
                coarse[first : first + WINDOW, (distance - 1) * width : distance * width],
                preferred_element_type=jnp.float32,
            ).astype(jnp.bfloat16)
        for distance in away:
            chip = jnp.bitwise_xor(place, distance)
            slots = pl.ds(pl.multiple_of(chip * width, width), width)
            copy = pltpu.make_async_copy(
                result.at[distance - 1, v], out_hbm.at[v, :, slots], sems.at[distance - 1, v]
            )
            copy.start()
            copies.append(copy)
    for copy in copies:
        copy.wait()


def exchange(array, distance):
    count = lax.axis_size("edge")
    return lax.ppermute(array, "edge", [(i, i ^ distance) for i in range(count)])


def across_sides(array):
    sides, count = lax.axis_size("side"), lax.axis_size("edge")
    moves = [
        (s * count + e, (s + (1 if e % 2 else -1)) % sides * count + e)
        for s in range(sides)
        for e in range(count)
    ]
    return lax.ppermute(array, AXES, moves)


def kernel_body(parent_blocks, interp_weight, tile_source, destination, remap_matrix):
    edge_count = lax.axis_size("edge")
    block_count = lax.axis_size(AXES)
    tiles, _, pcol, tile_rows = interp_weight.shape
    features = parent_blocks.shape[1]
    variables, child_levels, levels = remap_matrix.shape
    capacity = 2 * destination.shape[0] // edge_count
    slots = edge_count * capacity
    chips = edge_count // 2
    bf16 = jnp.bfloat16

    def cost(flops, bytes_accessed):
        return pl.CostEstimate(flops=flops, bytes_accessed=bytes_accessed, transcendentals=0)

    far = exchange(parent_blocks, 4)
    near = exchange(parent_blocks, 2)
    height = 2 * pcol + 8
    outbox, on_chip, given = pl.pallas_call(
        functools.partial(select_kernel, (edge_count, capacity, block_count)),
        out_shape=(
            jax.ShapeDtypeStruct((edge_count, height, capacity), bf16),
            jax.ShapeDtypeStruct((height, capacity), bf16),
            jax.ShapeDtypeStruct((height, capacity), bf16),
        ),
        in_specs=[HBM, HBM, HBM],
        out_specs=(VMEM, VMEM, VMEM),
        scratch_shapes=[
            pltpu.SMEM((2, tiles), jnp.int32),
            pltpu.VMEM((tiles, tile_rows), jnp.int32),
            pltpu.VMEM(interp_weight.shape, bf16),
            pltpu.VMEM((2 * pcol + 16, tiles * tile_rows), bf16),
            pltpu.SemaphoreType.DMA((3,)),
        ],
        cost_estimate=cost(2 * height * tiles * tile_rows * slots, 2 * height * slots),
        name="select_weights",
    )(tile_source.T, destination.reshape(tiles, tile_rows), interp_weight)
    block_bytes = 2 * features * pcol
    laid = pl.pallas_call(
        lay_remap_kernel,
        out_shape=jax.ShapeDtypeStruct((variables, child_levels, WINDOW), bf16),
        in_specs=[VMEM],
        out_specs=VMEM,
        compiler_params=ROOM,
        cost_estimate=cost(0, 4 * variables * child_levels * levels),
        name="lay_remap",
    )(jnp.swapaxes(remap_matrix, 1, 2))
    last = exchange(parent_blocks, 6)
    near = pl.pallas_call(
        pass_kernel,
        out_shape=jax.ShapeDtypeStruct(near.shape, bf16),
        in_specs=[ANY],
        out_specs=ANY,
        input_output_aliases={0: 0},
        compiler_params=ROOM,
        cost_estimate=cost(10**10, 10**9),
        name="behind_near",
    )(near)
    near, outbox = lax.optimization_barrier((near, outbox))
    inbox = lax.all_to_all(outbox, "edge", split_axis=0, concat_axis=0, tiled=True)
    held, rim = pl.pallas_call(
        collect_kernel,
        out_shape=(
            jax.ShapeDtypeStruct((chips, features, pcol), bf16),
            jax.ShapeDtypeStruct((1, features, pcol), bf16),
        ),
        in_specs=[VMEM] * 4,
        out_specs=(VMEM, VMEM),
        compiler_params=ROOM,
        cost_estimate=cost(10**11, 90000 * block_bytes),
        name="collect",
    )(parent_blocks, near, far, last)
    held, given = lax.optimization_barrier((held, given))
    rim = across_sides(rim)
    other = exchange(held, 1)
    other_rim = exchange(rim, 1)
    crossed = exchange(given, 1)
    padded = -(-features // 16) * 16
    parents, begun = pl.pallas_call(
        begin_kernel,
        out_shape=(
            jax.ShapeDtypeStruct((padded, (edge_count + 2) * pcol), bf16),
            jax.ShapeDtypeStruct((variables, child_levels, slots), bf16),
        ),
        in_specs=[VMEM] * 7,
        out_specs=(VMEM, HBM),
        scratch_shapes=[
            pltpu.VMEM((padded, 2 * capacity), bf16),
            pltpu.VMEM((variables, child_levels, 2 * capacity), bf16),
            pltpu.SemaphoreType.DMA((variables,)),
        ],
        compiler_params=ROOM,
        cost_estimate=cost(
            4 * capacity * (4 * pcol * features + variables * child_levels * levels),
            2 * variables * child_levels * slots,
        ),
        name="begin",
    )(on_chip, crossed, held, rim, other, other_rim, laid)
    away = slots - 2 * capacity
    return pl.pallas_call(
        functools.partial(finish_kernel, levels),
        out_shape=jax.ShapeDtypeStruct((variables, child_levels, slots), bf16),
        in_specs=[VMEM] * 3 + [HBM],
        out_specs=HBM,
        scratch_shapes=[
            pltpu.VMEM((padded, away), bf16),
            pltpu.VMEM((chips - 1, variables, child_levels, 2 * capacity), bf16),
            pltpu.SemaphoreType.DMA((chips - 1, variables)),
        ],
        input_output_aliases={3: 0},
        compiler_params=ROOM,
        cost_estimate=cost(
            2 * away * (4 * pcol * features + variables * child_levels * levels),
            2 * variables * child_levels * slots,
        ),
        name="finish",
    )(inbox, parents, laid, begun)


def plain_body(parent_blocks, interp_weight, tile_source, destination, remap_matrix):
    edge_count = lax.axis_size("edge")
    block_count = lax.axis_size(AXES)
    position = lax.axis_index(AXES)
    before, after = neighbours(parent_blocks)
    rim_blocks = jnp.concatenate([before, parent_blocks, after], axis=0)
    offset = (tile_source - position + 1 + block_count) % block_count
    chosen = rim_blocks[offset]
    summed = jnp.einsum(
        "tkfp,tkpr->tfr", chosen, interp_weight, preferred_element_type=jnp.float32
    )
    coarse = summed.astype(jnp.bfloat16)
    tile_count, feat_count, tile_rows = coarse.shape
    rows = coarse.transpose(1, 0, 2).reshape(feat_count, tile_count * tile_rows)
    row_count = destination.shape[0]
    capacity = max(2, 2 * row_count // edge_count)
    owners = destination[:, 0]
    owner_hits = (owners[:, None] == jnp.arange(edge_count, dtype=jnp.int32)[None, :]).astype(
        jnp.int32
    )
    places = jnp.sum(jnp.cumsum(owner_hits, axis=0) * owner_hits, axis=1) - 1
    slot_index = owners * capacity + places
    outbox = (
        jnp.zeros((feat_count, edge_count * capacity), jnp.bfloat16).at[:, slot_index].set(rows)
    )
    inbox = lax.all_to_all(outbox, "edge", split_axis=1, concat_axis=1, tiled=True)
    shaped = inbox.reshape(remap_matrix.shape[0], remap_matrix.shape[2], inbox.shape[1])
    result = jnp.einsum("vcl,vln->vcn", remap_matrix, shaped, preferred_element_type=jnp.float32)
    return result.astype(jnp.bfloat16)


def solution(mesh):
    body = kernel_body if mesh.shape["edge"] == 8 else plain_body
    return jax.shard_map(
        body,
        mesh=mesh,
        in_specs=(
            P(AXES, None, None),
            P(AXES, None, None, None),
            P(AXES, None),
            P(AXES, None),
            P(),
        ),
        out_specs=P(None, None, AXES),
        check_vma=False,
    )
```
